128 devices in a mesh: row: 16 (over y, x), col: 8 (over z, core).
Axes of the slice: x: 4, y: 4, z: 4, core: 2. Of those that a mesh axis runs over, the one named last changes fastest.
Arguments:
- elevation: float32 [16384, 16384], P('row', 'col'), may hold values from -12 to 12
- source_row: int32 [2048, 1], P(('row', 'col')), may hold values from 0 to 15, as said below
- source_block: int32 [2048, 1], P(('row', 'col')), may hold values from 0 to 31, as said below
- row_weights: bfloat16 [2048, 256, 256], P(('row', 'col')), may hold values from 0 to 1, as said below
- col_weights: bfloat16 [2048, 256, 256], P(('row', 'col')), may hold values from 0 to 1, as said below
Outputs:
- mercator: float32 [8192, 16384], P('row', 'col')
- overview_one: float32 [4096, 8192], P('row', 'col')
- overview_two: float32 [16, 8, 256, 256], P('row', 'col')
The draws below stay inside these ranges and needn't reach their ends.
Inputs may be any that keep to these rules, and one draw needn't show every extreme that they name: source_row[t] differs from the row index of t's own device by at most one; the targets of one device that share a tile row name the same value. The targets of one device that share a tile row name the same block row, source_block // 8; the block column source_block % (8) differs by at most one from (j % 8) (8) // 8, where j is the target's slot on its device. `row_weights`: entry (t, i, k) is zero unless k is (254) i // 255 or one more; those two entries lie in [0, 1] and sum to one up to bfloat16 rounding. `col_weights`: entry (t, k, l) is zero unless k is (254) l // 255 or one more; those two entries lie in [0, 1] and sum to one up to bfloat16 rounding.
All inputs are finite; a program needn't handle non-finite values.
Results may differ from the reference program's by a relative error of at most 0.0033.
Values may be sent and summed in bfloat16 or wider, within the bound.
A program may use at most 512 MiB of HBM per device.

```python
import math
import jax
import jax.numpy as jnp
from jax import lax

B = 256
CR = 1024
CC = 2048
TR_DEV = 2
TC_DEV = 8
TGT_DEV = 16
TARGETS = 2048
NR = 16384
NC = 16384
N_ROW = 16
N_COL = 8


def banded_weights(key, flipped):
    fraction = jax.random.uniform(key, (TARGETS, B), jnp.float32)
    positions = jnp.arange(B, dtype=jnp.int32) * (B - 2) // (B - 1)
    columns = jnp.arange(B, dtype=jnp.int32)
    hit_low = positions[:, None] == columns[None, :]
    hit_high = positions[:, None] + 1 == columns[None, :]
    dense = jnp.where(hit_low[None], 1.0 - fraction[:, :, None], 0.0) + jnp.where(hit_high[None], fraction[:, :, None], 0.0)
    if flipped:
        dense = jnp.swapaxes(dense, 1, 2)
    return dense.astype(jnp.float32)


def draw_row_weights(key, part):
    return banded_weights(jax.random.fold_in(key, 11), False).astype(jnp.bfloat16)


def draw_col_weights(key, part):
    return banded_weights(jax.random.fold_in(key, 23), True).astype(jnp.bfloat16)


def draw_source_row(key, part):
    group_count = TARGETS // TC_DEV
    moves = jax.random.randint(jax.random.fold_in(key, 5), (group_count,), -1, 2, dtype=jnp.int32)
    groups = jnp.arange(group_count, dtype=jnp.int32)
    device_row = groups // TR_DEV // N_COL
    moves = jnp.where(device_row == 0, 1, jnp.where(device_row == N_ROW - 1, -1, moves))
    return jnp.repeat(device_row + moves, TC_DEV).reshape(TARGETS, 1).astype(jnp.int32)


def draw_source_block(key, part):
    block_rows = CR // B
    block_cols = CC // B
    group_count = TARGETS // TC_DEV
    picked_rows = jax.random.randint(jax.random.fold_in(key, 7), (group_count,), 0, block_rows, dtype=jnp.int32)
    picked_rows = jnp.repeat(picked_rows, TC_DEV)
    slot_cols = jnp.arange(TARGETS, dtype=jnp.int32) % TC_DEV
    jitter = jax.random.randint(jax.random.fold_in(key, 9), (TARGETS,), -1, 2, dtype=jnp.int32)
    picked_cols = jnp.clip(slot_cols * block_cols // TC_DEV + jitter, 0, block_cols - 1)
    return (picked_rows * block_cols + picked_cols).reshape(TARGETS, 1).astype(jnp.int32)


def block_levels(own_key, shape, cuts, smallest, top_value):
    gain = 1.0
    for dim, parts in cuts:
        heights = jax.random.uniform(jax.random.fold_in(jax.random.fold_in(own_key, 6), dim), (parts,), jnp.float32, smallest / len(cuts), top_value / len(cuts))
        gain = gain * jnp.repeat(jnp.exp(heights), shape[dim] // parts).reshape((-1,) + (1,) * (len(shape) - 1 - dim))
    return gain


def bell_draw(key, shape, width, limit, cuts=(), kind=jnp.bfloat16):
    result = jax.random.normal(key, shape, jnp.float32) * width
    if len(cuts) > 0:
        result = block_levels(key, shape, cuts, -0.22, 0.18) * result
    return jnp.clip(result, min=-limit, max=limit).astype(kind)


def setup_inputs(seed: int = 0) -> dict:
    key_of = jax.random.split(jax.random.key(seed), 6)
    return {
        "elevation": bell_draw(key_of[0], (NR, NC), 2.0, 12.0, ((0, 16), (1, 8)), jnp.float32),
        "source_row": draw_source_row(jax.random.fold_in(key_of[5], 71), 0),
        "source_block": draw_source_block(jax.random.fold_in(key_of[5], 71), 0),
        "row_weights": draw_row_weights(jax.random.fold_in(key_of[5], 71), 0),
        "col_weights": draw_col_weights(jax.random.fold_in(key_of[5], 71), 0),
    }


SUN_COS = math.cos(math.pi / 4.0)
SUN_SIN = math.sin(math.pi / 4.0)
AZIMUTH_ANGLES = (1.25 * math.pi, 1.5 * math.pi, 1.75 * math.pi, 2.0 * math.pi)

def shade(padded):
    upper_left = padded[..., :-2, :-2]
    upper_mid = padded[..., :-2, 1:-1]
    upper_right = padded[..., :-2, 2:]
    middle_left = padded[..., 1:-1, :-2]
    middle_right = padded[..., 1:-1, 2:]
    lower_left = padded[..., 2:, :-2]
    lower_mid = padded[..., 2:, 1:-1]
    lower_right = padded[..., 2:, 2:]
    east_slope = (upper_right + 2.0 * middle_right + lower_right - (upper_left + 2.0 * middle_left + lower_left)) * 0.125
    south_slope = (lower_left + 2.0 * lower_mid + lower_right - (upper_left + 2.0 * upper_mid + upper_right)) * 0.125
    scale_back = 1.0 / jnp.sqrt(1.0 + east_slope * east_slope + south_slope * south_slope)
    lit_total = jnp.zeros_like(east_slope)
    for azimuth in AZIMUTH_ANGLES:
        along_light = east_slope * math.sin(azimuth) - south_slope * math.cos(azimuth)
        lit_total = lit_total + jnp.maximum(SUN_COS - SUN_SIN * along_light, 0.0)
    return 0.25 * lit_total * scale_back

def halve_image(picture):
    pic_rows, pic_cols = picture.shape
    return lax.optimization_barrier(jnp.sum(picture.reshape(pic_rows // 2, 2, pic_cols // 2, 2), axis=(1, 3))) * 0.25

def render(pieces):
    src_piece, left_piece, right_piece = pieces
    inner_rows = jnp.einsum('tik,tkl->til', left_piece.astype(jnp.float32), src_piece.astype(jnp.float32)).astype(jnp.bfloat16)
    inner_rows = lax.optimization_barrier(inner_rows)
    return jnp.einsum('tik,tkl->til', inner_rows.astype(jnp.float32), right_piece.astype(jnp.float32))

def reference(elevation, source_row, source_block, row_weights, col_weights):
    shaded = shade(jnp.pad(elevation, 1)).astype(jnp.bfloat16)
    block_rows = CR // B
    block_cols = CC // B
    grid_blocks = shaded.reshape(NR // B, B, NC // B, B).transpose(0, 2, 1, 3)
    target_ids = jnp.arange(TARGETS, dtype=jnp.int32)
    device_col = target_ids // TGT_DEV % N_COL
    global_row = source_row[:, 0] * block_rows + source_block[:, 0] // block_cols
    global_col = device_col * block_cols + source_block[:, 0] % block_cols
    sources = grid_blocks[global_row, global_col]
    tile_stack = lax.map(render, (sources.reshape(-1, TGT_DEV, B, B), row_weights.reshape(-1, TGT_DEV, B, B), col_weights.reshape(-1, TGT_DEV, B, B)))
    mercator = tile_stack.reshape(N_ROW, N_COL, TR_DEV, TC_DEV, B, B).transpose(0, 2, 4, 1, 3, 5).reshape(N_ROW * TR_DEV * B, N_COL * TC_DEV * B)
    overview_one = halve_image(mercator)
    level_two = halve_image(overview_one)
    coarse_tiles = level_two.reshape(N_ROW // 2, B, 2 * N_COL, B).transpose(0, 2, 1, 3)
    overview_two = coarse_tiles.reshape(N_ROW // 2, N_COL, 2, B, B).transpose(0, 2, 1, 3, 4).reshape(N_ROW, N_COL, B, B)
    return (mercator, overview_one, overview_two)
```

```python
import functools
import math

import jax
import jax.numpy as jnp
from jax import lax
from jax.experimental import pallas as pl
from jax.experimental.pallas import tpu as pltpu
from jax.sharding import PartitionSpec as P

B = 256
HALF = B // 2
TR_DEV = 2
TC_DEV = 8
PAD_R = 8
PAD_C = 128
BAND = 32
ORDER = (1, 2, 3, 4, 0, 5, 6, 7)
READY = ((), (), (2,), (3,), (0, 1), (4,), (5,), (6, 7))

SUN_COS = math.cos(math.pi / 4.0)
MESH = pl.DeviceIdType.MESH


def lit_of(east, south):
    base = 0.25 * SUN_COS
    straight = base / 8.0
    slanted = 0.25 * 0.5 / 8.0
    scale = lax.rsqrt(1.0 + (east * east + south * south) * (1.0 / 64.0))
    lit = jnp.maximum(base + (east - south) * slanted, 0.0)
    lit = lit + jnp.maximum(base + east * straight, 0.0)
    lit = lit + jnp.maximum(base + (east + south) * slanted, 0.0)
    lit = lit + jnp.maximum(base + south * straight, 0.0)
    return lit * scale


def chosen(index, options):
    value = options[0]
    for k, option in enumerate(options[1:], 1):
        value = jnp.where(index == k, option, value)
    return value


def pooled(both, pool):
    high = both.astype(jnp.bfloat16)
    low = (both - high.astype(jnp.float32)).astype(jnp.bfloat16)
    return jnp.dot(high, pool, preferred_element_type=jnp.float32) + jnp.dot(
        low, pool, preferred_element_type=jnp.float32
    )


def kernel(
    n_row, n_col,
    ask_ref, ask_hbm, elev_hbm, roww_hbm, colw_hbm,
    merc_hbm, one_hbm, two_hbm,
    padded, shaded, asked, asked_s, sendbuf, merged, roww, colw, tiles, ones, two_own, two_send, two_got,
    *rest,
):
    recv = rest[:16]
    (load_sem, ask_send, ask_recv, ask_local, halo_send, halo_recv,
     strip_send, strip_recv, two_sems, out_sem) = rest[16:]
    row = lax.axis_index("row")
    col = lax.axis_index("col")
    rows, cols = elev_hbm.shape
    parity = lax.rem(row, 2)
    up = lax.rem(row + n_row - 1, n_row)
    down = lax.rem(row + 1, n_row)
    left = lax.rem(col + n_col - 1, n_col)
    right = lax.rem(col + 1, n_col)
    last = TC_DEV - 1

    def sent_col(m):
        return m + parity * (last - 2 * m)

    def got_col(m):
        return (last - m) + parity * (2 * m - last)

    inner = padded.at[pl.ds(PAD_R, rows), pl.ds(PAD_C, cols)]
    load_elev = pltpu.make_async_copy(elev_hbm, inner, load_sem.at[0])
    load_elev.start()

    around = [(up, col), (down, col), (row, left), (row, right), (up, left), (up, right), (down, left), (down, right)]
    barrier = pltpu.get_barrier_semaphore()
    for device in around:
        pl.semaphore_signal(barrier, inc=1, device_id=device, device_id_type=MESH)
    pl.semaphore_wait(barrier, len(around))

    def remote(src, dst, send_sem, recv_sem, device):
        return pltpu.make_async_remote_copy(
            src_ref=src, dst_ref=dst, send_sem=send_sem, recv_sem=recv_sem, device_id=device, device_id_type=MESH
        )

    asks = [
        remote(ask_hbm, asked.at[1], ask_send.at[0], ask_recv.at[1], (up, col)),
        remote(ask_hbm, asked.at[0], ask_send.at[1], ask_recv.at[0], (down, col)),
    ]
    for copy in asks:
        copy.start()

    top, bottom = pl.ds(0, PAD_R), pl.ds(PAD_R + rows, PAD_R)
    mid_r, mid_c = pl.ds(PAD_R, rows), pl.ds(PAD_C, cols)
    west, east = pl.ds(0, PAD_C), pl.ds(PAD_C + cols, PAD_C)
    first_r, last_r = pl.ds(0, PAD_R), pl.ds(rows - PAD_R, PAD_R)
    first_c, last_c = pl.ds(0, PAD_C), pl.ds(cols - PAD_C, PAD_C)
    all_r, all_c = pl.ds(0, rows), pl.ds(0, cols)
    halo_plan = [
        ((first_r, all_c), (bottom, mid_c), (up, col)),
        ((last_r, all_c), (top, mid_c), (down, col)),
        ((all_r, first_c), (mid_r, east), (row, left)),
        ((all_r, last_c), (mid_r, west), (row, right)),
        ((first_r, first_c), (bottom, east), (up, left)),
        ((first_r, last_c), (bottom, west), (up, right)),
        ((last_r, first_c), (top, east), (down, left)),
        ((last_r, last_c), (top, west), (down, right)),
    ]
    halos = [
        remote(elev_hbm.at[src], padded.at[dst], halo_send.at[i], halo_recv.at[i], device)
        for i, (src, dst, device) in enumerate(halo_plan)
    ]
    for copy in halos:
        copy.start()
    load_roww = pltpu.make_async_copy(roww_hbm, roww, load_sem.at[1])
    load_colw = pltpu.make_async_copy(colw_hbm, colw, load_sem.at[2])
    load_roww.start()
    load_colw.start()

    for copy in asks:
        copy.wait_recv()
    to_scalar = pltpu.make_async_copy(asked, asked_s, ask_local)
    to_scalar.start()
    load_elev.wait()
    halos[0].wait_recv()
    halos[1].wait_recv()

    def clear(where):
        shape = tuple(s.size for s in where)
        padded[where] = jnp.zeros(shape, jnp.float32)

    @pl.when(row == 0)
    def _():
        clear((top, mid_c))

    @pl.when(row == n_row - 1)
    def _():
        clear((bottom, mid_c))

    to_scalar.wait()

    pool_rows = lax.broadcasted_iota(jnp.int32, (B, HALF), 0)
    pool_cols = lax.broadcasted_iota(jnp.int32, (B, HALF), 1)
    pool = jnp.where(pool_rows // 2 == pool_cols, 0.25, 0.0).astype(jnp.bfloat16)

    strips = []
    for step, m in enumerate(ORDER):
        if step == 4:
            for copy in halos[2:]:
                copy.wait_recv()

            @pl.when(col == 0)
            def _():
                clear((mid_r, west))

            @pl.when(col == n_col - 1)
            def _():
                clear((mid_r, east))

            @pl.when((row == 0) | (col == 0))
            def _():
                clear((top, west))

            @pl.when((row == 0) | (col == n_col - 1))
            def _():
                clear((top, east))

            @pl.when((row == n_row - 1) | (col == 0))
            def _():
                clear((bottom, west))

            @pl.when((row == n_row - 1) | (col == n_col - 1))
            def _():
                clear((bottom, east))

        lane = pl.multiple_of(sent_col(m) * B, PAD_C)
        slot = step % 2

        def shade_band(i, carry, lane=lane, slot=slot):
            start = pl.multiple_of(i * BAND, BAND)
            cells = padded[pl.ds(start, BAND + 2 * PAD_R), pl.ds(lane, B + 2 * PAD_C)]
            before = cells[:, PAD_C - 1 : PAD_C - 1 + B]
            here = cells[:, PAD_C : PAD_C + B]
            after = cells[:, PAD_C + 1 : PAD_C + 1 + B]
            across = after - before
            along = (before + after) + (here + here)
            middle = across[PAD_R : PAD_R + BAND]
            east8 = (across[PAD_R - 1 : PAD_R - 1 + BAND] + across[PAD_R + 1 : PAD_R + 1 + BAND]) + (middle + middle)
            south8 = along[PAD_R + 1 : PAD_R + 1 + BAND] - along[PAD_R - 1 : PAD_R - 1 + BAND]
            shaded[slot, pl.ds(start, BAND), :] = lit_of(east8, south8).astype(jnp.bfloat16)
            return carry

        lax.fori_loop(0, rows // BAND, shade_band, 0)
        for g in range(TR_DEV):
            for side in range(2):
                sendbuf[side, m, g] = chosen(
                    lax.div(asked_s[side, 1, g * TC_DEV], TC_DEV),
                    [shaded[slot, k * B : (k + 1) * B, :] for k in range(rows // B)],
                )
        for g in range(TR_DEV):
            for side, (device, place) in enumerate((((up, col), 2), ((down, col), 0))):
                copy = remote(
                    sendbuf.at[side, m, g],
                    recv[m * TR_DEV + g].at[place],
                    strip_send.at[side, m, g],
                    strip_recv.at[side, m, g],
                    device,
                )
                copy.start()
                strips.append(((step, g, side), copy))
        for g in range(TR_DEV):
            recv[(last - m) * TR_DEV + g][1] = chosen(
                lax.div(ask_ref[1, g * TC_DEV], TC_DEV),
                [shaded[slot, k * B : (k + 1) * B, :] for k in range(rows // B)],
            )
    strips = dict(strips)

    load_roww.wait()
    load_colw.wait()
    outs = []
    two_copy = remote(two_send, two_got, two_sems.at[0], two_sems.at[1], (row + 1 - 2 * parity, col))

    def out_copy(src, dst):
        copy = pltpu.make_async_copy(src, dst, out_sem.at[len(outs)])
        copy.start()
        outs.append(copy)

    def make_target(g, m):
        j = got_col(m)
        t = g * TC_DEV + j
        place = g * TC_DEV + m
        near = [k for k in (m - 1, m, m + 1) if 0 <= k <= last]
        wanted = lax.rem(ask_ref[1, t], TC_DEV)
        where = wanted + (1 - parity) * (last - 2 * wanted)
        source = chosen(where - near[0], [merged[g, k] for k in near])
        half_done = jnp.dot(roww[t], source, preferred_element_type=jnp.float32).astype(jnp.bfloat16)
        tile = jnp.dot(half_done, colw[t], preferred_element_type=jnp.float32)
        sums = []
        for half in range(2):
            tiles[place, half] = tile[:, half * HALF : (half + 1) * HALF]
            lane = pl.multiple_of(j * B + half * HALF, HALF)
            out_copy(tiles.at[place, half], merc_hbm.at[pl.ds(g * B, B), pl.ds(lane, HALF)])
            sums.append(tiles[place, half, pl.ds(0, HALF, stride=2), :] + tiles[place, half, pl.ds(1, HALF, stride=2), :])
        where = (g * 4 + m // 2, lax.rem(j, 2))
        ones[where] = pooled(jnp.concatenate(sums, axis=1), pool)
        lane = pl.multiple_of(j * HALF, HALF)
        out_copy(ones.at[where], one_hbm.at[pl.ds(g * HALF, HALF), pl.ds(lane, HALF)])

    def make_coarse(g, pair):
        actual = lax.div(got_col(2 * pair), 2)
        quarter = HALF // 2
        sums = [
            ones[g * 4 + pair, half, pl.ds(0, quarter, stride=2), :] + ones[g * 4 + pair, half, pl.ds(1, quarter, stride=2), :]
            for half in range(2)
        ]
        lane = pl.multiple_of(lax.rem(actual, 2) * HALF, HALF)
        dest = two_send if pair < 2 else two_own
        dest[pl.ds(g * quarter, quarter), pl.ds(lane, HALF)] = pooled(jnp.concatenate(sums, axis=1), pool)

    done = set()
    for step, m in enumerate(ORDER):
        for g in range(TR_DEV):
            strips[step, g, 0].wait_recv()
            strips[step, g, 1].wait_recv()
            side = ask_ref[0, g * TC_DEV] - row + 1
            merged[g, m] = chosen(side, [recv[m * TR_DEV + g][k] for k in range(3)])
            for target in READY[step]:
                make_target(g, target)
                done.add((g, target))
                pair = target // 2
                if (g, 2 * pair) in done and (g, 2 * pair + 1) in done:
                    make_coarse(g, pair)
        if step == 4:
            two_copy.start()
    out_copy(two_own, two_hbm.at[pl.ds(pl.multiple_of(parity * (HALF), HALF), HALF), :])
    two_copy.wait_recv()
    out_copy(two_got, two_hbm.at[pl.ds(pl.multiple_of((1 - parity) * (HALF), HALF), HALF), :])
    for copy in outs:
        copy.wait()
    two_copy.wait_send()
    for copy in asks + halos + list(strips.values()):
        copy.wait_send()


def per_device(n_row, n_col, elevation, source_row, source_block, row_weights, col_weights):
    rows, cols = elevation.shape
    targets = source_row.shape[0]
    ask = jnp.zeros((8, 128), jnp.int32)
    ask = lax.dynamic_update_slice(ask, source_row.reshape(1, targets), (0, 0))
    ask = lax.dynamic_update_slice(ask, source_block.reshape(1, targets), (1, 0))
    anywhere = pl.BlockSpec(memory_space=pl.ANY)
    vmem, bf16, f32 = pltpu.VMEM, jnp.bfloat16, jnp.float32
    dma = pltpu.SemaphoreType.DMA
    n_out = 3 * targets + 2
    mercator, one, two = pl.pallas_call(
        functools.partial(kernel, n_row, n_col),
        out_shape=(
            jax.ShapeDtypeStruct((TR_DEV * B, TC_DEV * B), f32),
            jax.ShapeDtypeStruct((TR_DEV * HALF, TC_DEV * HALF), f32),
            jax.ShapeDtypeStruct((B, B), f32),
        ),
        in_specs=[pl.BlockSpec(memory_space=pltpu.SMEM)] + [anywhere] * 4,
        out_specs=(anywhere,) * 3,
        scratch_shapes=[
            vmem((rows + 2 * PAD_R, cols + 2 * PAD_C), f32),
            vmem((2, rows, B), bf16),
            vmem((2, 8, 128), jnp.int32),
            pltpu.SMEM((2, 8, 128), jnp.int32),
            vmem((2, TC_DEV, TR_DEV, B, B), bf16),
            vmem((TR_DEV, TC_DEV, B, B), bf16),
            vmem((targets, B, B), bf16),
            vmem((targets, B, B), bf16),
            vmem((targets, 2, B, HALF), f32),
            vmem((targets // 2, 2, HALF, HALF), f32),
            vmem((HALF, B), f32),
            vmem((HALF, B), f32),
            vmem((HALF, B), f32),
        ]
        + [vmem((3, B, B), bf16)] * targets
        + [
            dma((3,)), dma((2,)), dma((2,)), dma, dma((8,)), dma((8,)),
            dma((2, TC_DEV, TR_DEV)), dma((2, TC_DEV, TR_DEV)), dma((2,)), dma((n_out,)),
        ],
        compiler_params=pltpu.CompilerParams(
            collective_id=0, has_side_effects=True, vmem_limit_bytes=44 * 1024 * 1024
        ),
        name="hillshade_tiles",
    )(ask, ask, elevation, row_weights, col_weights)
    return mercator, one, two.reshape(1, 1, B, B)


def solution(mesh):
    in_specs = (
        P("row", "col"),
        P(("row", "col"), None),
        P(("row", "col"), None),
        P(("row", "col"), None, None),
        P(("row", "col"), None, None),
    )
    out_specs = (P("row", "col"), P("row", "col"), P("row", "col", None, None))
    return jax.shard_map(
        functools.partial(per_device, mesh.shape["row"], mesh.shape["col"]),
        mesh=mesh, in_specs=in_specs, out_specs=out_specs, check_vma=False,
    )
```

```python
import functools
import math

import jax
import jax.numpy as jnp
from jax import lax
from jax.experimental import pallas as pl
from jax.experimental.pallas import tpu as pltpu
from jax.sharding import PartitionSpec as P

B = 256
HALF = B // 2
TR_DEV = 2
TC_DEV = 8
PAD_R = 8
PAD_C = 128
BAND = 64
ORDER = (1, 2, 3, 4, 0, 5, 6, 7)
READY = ((), (), (2,), (3,), (0, 1), (4,), (5,), (6, 7))

SUN_COS = math.cos(math.pi / 4.0)
MESH = pl.DeviceIdType.MESH


def shade(cells, band):
    height, width = cells.shape
    beside = cells + pltpu.roll(cells, width - 1, 1)
    box = beside + pltpu.roll(beside, height - 1, 0)
    box_up = pltpu.roll(box, 1, 0)
    middle = slice(PAD_R, PAD_R + band), slice(PAD_C, width - PAD_C)
    one = box[middle] - pltpu.roll(box_up, 1, 1)[middle]
    two = box_up[middle] - pltpu.roll(box, 1, 1)[middle]
    scale = lax.rsqrt((one * one + two * two) * 32.0 + 1024.0)
    slanted = jnp.maximum(two, -8.0 * SUN_COS) + jnp.maximum(one, -8.0 * SUN_COS)
    straight = jnp.maximum(one + two, -8.0) + jnp.maximum(one - two, -8.0)
    return (straight * SUN_COS + (slanted + 32.0 * SUN_COS)) * scale


def chosen(index, options):
    value = options[0]
    for k, option in enumerate(options[1:], 1):
        value = jnp.where(index == k, option, value)
    return value


def pooled(both, pool):
    high = both.astype(jnp.bfloat16)
    low = (both - high.astype(jnp.float32)).astype(jnp.bfloat16)
    return jnp.dot(high, pool, preferred_element_type=jnp.float32) + jnp.dot(
        low, pool, preferred_element_type=jnp.float32
    )


def kernel(
    n_row, n_col,
    srow_hbm, ask_hbm, elev_hbm, roww_hbm, colw_hbm,
    merc_hbm, one_hbm, two_hbm,
    srow_ref, sblock_ref, padded, shaded, asked, asked_s, sendbuf, merged, roww, colw, tiles, ones, two_own, two_send, two_got,
    *rest,
):
    recv = rest[:16]
    (load_sem, ask_send, ask_recv, ask_local, halo_send, halo_recv,
     strip_send, strip_recv, two_sems, out_sem) = rest[16:]
    row = lax.axis_index("row")
    col = lax.axis_index("col")
    rows, cols = elev_hbm.shape
    parity = lax.rem(row, 2)
    up = lax.rem(row + n_row - 1, n_row)
    down = lax.rem(row + 1, n_row)
    left = lax.rem(col + n_col - 1, n_col)
    right = lax.rem(col + 1, n_col)
    last = TC_DEV - 1

    def sent_col(m):
        return m + parity * (last - 2 * m)

    def got_col(m):
        return (last - m) + parity * (2 * m - last)

    def load_block(m):
        lane = pl.multiple_of(sent_col(m) * B, B)
        return pltpu.make_async_copy(
            elev_hbm.at[:, pl.ds(lane, B)],
            padded.at[pl.ds(PAD_R, rows), pl.ds(lane + PAD_C, B)],
            load_sem.at[m],
        )

    loads = {m: load_block(m) for m in (1, 0, 2, 3, 4, 5, 6, 7)}
    for copy in loads.values():
        copy.start()

    numbers = [
        pltpu.make_async_copy(srow_hbm, srow_ref, ask_local.at[1]),
        pltpu.make_async_copy(ask_hbm, sblock_ref, ask_local.at[2]),
    ]
    for copy in numbers:
        copy.start()

    around = [(up, col), (down, col), (row, left), (row, right), (up, left), (up, right), (down, left), (down, right)]
    barrier = pltpu.get_barrier_semaphore()
    for device in around:
        pl.semaphore_signal(barrier, inc=1, device_id=device, device_id_type=MESH)
    pl.semaphore_wait(barrier, len(around))

    def remote(src, dst, send_sem, recv_sem, device):
        return pltpu.make_async_remote_copy(
            src_ref=src, dst_ref=dst, send_sem=send_sem, recv_sem=recv_sem, device_id=device, device_id_type=MESH
        )

    asks = [
        remote(ask_hbm, asked.at[1], ask_send.at[0], ask_recv.at[1], (up, col)),
        remote(ask_hbm, asked.at[0], ask_send.at[1], ask_recv.at[0], (down, col)),
    ]
    for copy in asks:
        copy.start()

    top, bottom = pl.ds(0, PAD_R), pl.ds(PAD_R + rows, PAD_R)
    mid_r, mid_c = pl.ds(PAD_R, rows), pl.ds(PAD_C, cols)
    west, east = pl.ds(0, PAD_C), pl.ds(PAD_C + cols, PAD_C)
    first_r, last_r = pl.ds(0, PAD_R), pl.ds(rows - PAD_R, PAD_R)
    first_c, last_c = pl.ds(0, PAD_C), pl.ds(cols - PAD_C, PAD_C)
    all_r, all_c = pl.ds(0, rows), pl.ds(0, cols)
    halo_plan = [
        ((first_r, all_c), (bottom, mid_c), (up, col)),
        ((last_r, all_c), (top, mid_c), (down, col)),
        ((all_r, first_c), (mid_r, east), (row, left)),
        ((all_r, last_c), (mid_r, west), (row, right)),
        ((first_r, first_c), (bottom, east), (up, left)),
        ((first_r, last_c), (bottom, west), (up, right)),
        ((last_r, first_c), (top, east), (down, left)),
        ((last_r, last_c), (top, west), (down, right)),
    ]
    halos = [
        remote(elev_hbm.at[src], padded.at[dst], halo_send.at[i], halo_recv.at[i], device)
        for i, (src, dst, device) in enumerate(halo_plan)
    ]
    for copy in halos:
        copy.start()
    load_roww = pltpu.make_async_copy(roww_hbm, roww, load_sem.at[TC_DEV])
    load_colw = pltpu.make_async_copy(colw_hbm, colw, load_sem.at[TC_DEV + 1])
    load_roww.start()
    load_colw.start()

    def clear(where):
        shape = tuple(s.size for s in where)
        padded[where] = jnp.zeros(shape, jnp.float32)

    def first_halo():
        for copy in asks:
            copy.wait_recv()
        to_scalar.start()
        halos[0].wait_recv()
        halos[1].wait_recv()

        @pl.when(row == 0)
        def _():
            clear((top, mid_c))

        @pl.when(row == n_row - 1)
        def _():
            clear((bottom, mid_c))

        for copy in [to_scalar] + numbers:
            copy.wait()

    to_scalar = pltpu.make_async_copy(asked, asked_s, ask_local.at[0])
    arrived = set()

    pool_rows = lax.broadcasted_iota(jnp.int32, (B, HALF), 0)
    pool_cols = lax.broadcasted_iota(jnp.int32, (B, HALF), 1)
    pool = jnp.where(pool_rows // 2 == pool_cols, 0.25, 0.0).astype(jnp.bfloat16)

    strips = []
    for step, m in enumerate(ORDER):
        if step == 4:
            for copy in halos[2:]:
                copy.wait_recv()

            @pl.when(col == 0)
            def _():
                clear((mid_r, west))

            @pl.when(col == n_col - 1)
            def _():
                clear((mid_r, east))

            @pl.when((row == 0) | (col == 0))
            def _():
                clear((top, west))

            @pl.when((row == 0) | (col == n_col - 1))
            def _():
                clear((top, east))

            @pl.when((row == n_row - 1) | (col == 0))
            def _():
                clear((bottom, west))

            @pl.when((row == n_row - 1) | (col == n_col - 1))
            def _():
                clear((bottom, east))

        lane = pl.multiple_of(sent_col(m) * B, PAD_C)
        slot = step % 2

        def shade_band(i, carry, lane=lane, slot=slot):
            start = pl.multiple_of(i * BAND, BAND)
            cells = padded[pl.ds(start, BAND + 2 * PAD_R), pl.ds(lane, B + 2 * PAD_C)]
            shaded[slot, pl.ds(start, BAND), :] = shade(cells, BAND).astype(jnp.bfloat16)
            return carry

        for k in (m - 1, m, m + 1):
            if 0 <= k <= last and k not in arrived:
                loads[k].wait()
                arrived.add(k)
        bands = rows // BAND
        if step == 0:
            lax.fori_loop(1, bands - 1, shade_band, 0, unroll=2)
            first_halo()
            lax.fori_loop(0, 2, lambda i, c: shade_band(i * (bands - 1), c), 0)
        else:
            lax.fori_loop(0, bands, shade_band, 0, unroll=2)
        for g in range(TR_DEV):
            for side in range(2):
                sendbuf[side, m, g] = chosen(
                    lax.div(asked_s[side, 0, g * TC_DEV], TC_DEV),
                    [shaded[slot, k * B : (k + 1) * B, :] for k in range(rows // B)],
                )
        for g in range(TR_DEV):
            for side, (device, place) in enumerate((((up, col), 2), ((down, col), 0))):
                copy = remote(
                    sendbuf.at[side, m, g],
                    recv[m * TR_DEV + g].at[place],
                    strip_send.at[side, m, g],
                    strip_recv.at[side, m, g],
                    device,
                )
                copy.start()
                strips.append(((step, g, side), copy))
        for g in range(TR_DEV):
            recv[(last - m) * TR_DEV + g][1] = chosen(
                lax.div(sblock_ref[0, g * TC_DEV], TC_DEV),
                [shaded[slot, k * B : (k + 1) * B, :] for k in range(rows // B)],
            )
    strips = dict(strips)

    load_roww.wait()
    load_colw.wait()
    outs = []
    two_copy = remote(two_send, two_got, two_sems.at[0], two_sems.at[1], (row + 1 - 2 * parity, col))

    def out_copy(src, dst):
        copy = pltpu.make_async_copy(src, dst, out_sem.at[len(outs)])
        copy.start()
        outs.append(copy)

    def make_target(g, m):
        j = got_col(m)
        t = g * TC_DEV + j
        place = g * TC_DEV + m
        near = [k for k in (m - 1, m, m + 1) if 0 <= k <= last]
        wanted = lax.rem(sblock_ref[0, t], TC_DEV)
        where = wanted + (1 - parity) * (last - 2 * wanted)
        source = chosen(where - near[0], [merged[g, k] for k in near])
        half_done = jnp.dot(roww[t], source, preferred_element_type=jnp.float32).astype(jnp.bfloat16)
        tile = jnp.dot(half_done, colw[t], preferred_element_type=jnp.float32)
        sums = []
        for half in range(2):
            tiles[place, half] = tile[:, half * HALF : (half + 1) * HALF]
            lane = pl.multiple_of(j * B + half * HALF, HALF)
            out_copy(tiles.at[place, half], merc_hbm.at[pl.ds(g * B, B), pl.ds(lane, HALF)])
            sums.append(tiles[place, half, pl.ds(0, HALF, stride=2), :] + tiles[place, half, pl.ds(1, HALF, stride=2), :])
        where = (g * 4 + m // 2, lax.rem(j, 2))
        ones[where] = pooled(jnp.concatenate(sums, axis=1), pool)
        lane = pl.multiple_of(j * HALF, HALF)
        out_copy(ones.at[where], one_hbm.at[pl.ds(g * HALF, HALF), pl.ds(lane, HALF)])

    def make_coarse(g, pair):
        actual = lax.div(got_col(2 * pair), 2)
        quarter = HALF // 2
        sums = [
            ones[g * 4 + pair, half, pl.ds(0, quarter, stride=2), :] + ones[g * 4 + pair, half, pl.ds(1, quarter, stride=2), :]
            for half in range(2)
        ]
        lane = pl.multiple_of(lax.rem(actual, 2) * HALF, HALF)
        dest = two_send if pair < 2 else two_own
        dest[pl.ds(g * quarter, quarter), pl.ds(lane, HALF)] = pooled(jnp.concatenate(sums, axis=1), pool)

    done = set()
    for step, m in enumerate(ORDER):
        for g in range(TR_DEV):
            strips[step, g, 0].wait_recv()
            strips[step, g, 1].wait_recv()
            side = srow_ref[0, g * TC_DEV] - row + 1
            merged[g, m] = chosen(side, [recv[m * TR_DEV + g][k] for k in range(3)])
            for target in READY[step]:
                make_target(g, target)
                done.add((g, target))
                pair = target // 2
                if (g, 2 * pair) in done and (g, 2 * pair + 1) in done:
                    make_coarse(g, pair)
        if step == 4:
            two_copy.start()
    out_copy(two_own, two_hbm.at[pl.ds(pl.multiple_of(parity * (HALF), HALF), HALF), :])
    two_copy.wait_recv()
    out_copy(two_got, two_hbm.at[pl.ds(pl.multiple_of((1 - parity) * (HALF), HALF), HALF), :])
    for copy in outs:
        copy.wait()
    two_copy.wait_send()
    for copy in asks + halos + list(strips.values()):
        copy.wait_send()


def per_device(n_row, n_col, elevation, source_row, source_block, row_weights, col_weights):
    rows, cols = elevation.shape
    targets = source_row.shape[0]
    source_row = source_row.reshape(1, targets)
    source_block = source_block.reshape(1, targets)
    anywhere = pl.BlockSpec(memory_space=pl.ANY)
    in_hbm = pl.BlockSpec(memory_space=pltpu.HBM)
    operands = (source_row, source_block, elevation, row_weights, col_weights)
    vmem, bf16, f32 = pltpu.VMEM, jnp.bfloat16, jnp.float32
    dma = pltpu.SemaphoreType.DMA
    n_out = 3 * targets + 2
    mercator, one, two = pl.pallas_call(
        functools.partial(kernel, n_row, n_col),
        out_shape=(
            jax.ShapeDtypeStruct((TR_DEV * B, TC_DEV * B), f32),
            jax.ShapeDtypeStruct((TR_DEV * HALF, TC_DEV * HALF), f32),
            jax.ShapeDtypeStruct((B, B), f32),
        ),
        in_specs=[in_hbm] * len(operands),
        out_specs=(anywhere,) * 3,
        scratch_shapes=[
            pltpu.SMEM((1, targets), jnp.int32),
            pltpu.SMEM((1, targets), jnp.int32),
            vmem((rows + 2 * PAD_R, cols + 2 * PAD_C), f32),
            vmem((2, rows, B), bf16),
            vmem((2, 1, targets), jnp.int32),
            pltpu.SMEM((2, 1, targets), jnp.int32),
            vmem((2, TC_DEV, TR_DEV, B, B), bf16),
            vmem((TR_DEV, TC_DEV, B, B), bf16),
            vmem((targets, B, B), bf16),
            vmem((targets, B, B), bf16),
            vmem((targets, 2, B, HALF), f32),
            vmem((targets // 2, 2, HALF, HALF), f32),
            vmem((HALF, B), f32),
            vmem((HALF, B), f32),
            vmem((HALF, B), f32),
        ]
        + [vmem((3, B, B), bf16)] * targets
        + [
            dma((TC_DEV + 2,)), dma((2,)), dma((2,)), dma((3,)), dma((8,)), dma((8,)),
            dma((2, TC_DEV, TR_DEV)), dma((2, TC_DEV, TR_DEV)), dma((2,)), dma((n_out,)),
        ],
        compiler_params=pltpu.CompilerParams(
            collective_id=0, has_side_effects=True, vmem_limit_bytes=44 * 1024 * 1024
        ),
        name="hillshade_tiles",
    )(*(pltpu.with_memory_space_constraint(x, pltpu.HBM) for x in operands))
    return mercator, one, two.reshape(1, 1, B, B)


def solution(mesh):
    in_specs = (
        P("row", "col"),
        P(("row", "col"), None),
        P(("row", "col"), None),
        P(("row", "col"), None, None),
        P(("row", "col"), None, None),
    )
    out_specs = (P("row", "col"), P("row", "col"), P("row", "col", None, None))
    return jax.shard_map(
        functools.partial(per_device, mesh.shape["row"], mesh.shape["col"]),
        mesh=mesh, in_specs=in_specs, out_specs=out_specs, check_vma=False,
    )
```

```python
import functools
import math

import jax
import jax.numpy as jnp
from jax import lax
from jax.experimental import pallas as pl
from jax.experimental.pallas import tpu as pltpu
from jax.sharding import PartitionSpec as P

B = 256
HALF = B // 2
QUARTER = B // 4
TR_DEV = 2
TC_DEV = 8
PAD_R = 8
PAD_C = 128
BAND = 64
ORDER = (1, 2, 3, 4, 0, 5, 6, 7)
READY = ((), (), (2,), (3,), (0, 1), (4,), (5,), (6, 7))
LATE = ((1, 6), (1, 7))

SUN_COS = math.cos(math.pi / 4.0)
MESH = pl.DeviceIdType.MESH


def shade(cells, band):
    height, width = cells.shape
    beside = cells + pltpu.roll(cells, width - 1, 1)
    box = beside + pltpu.roll(beside, height - 1, 0)
    box_up = pltpu.roll(box, 1, 0)
    middle = slice(PAD_R, PAD_R + band), slice(PAD_C, width - PAD_C)
    one = box[middle] - pltpu.roll(box_up, 1, 1)[middle]
    two = box_up[middle] - pltpu.roll(box, 1, 1)[middle]
    scale = lax.rsqrt((one * one + two * two) * 32.0 + 1024.0)
    slanted = jnp.maximum(two, -8.0 * SUN_COS) + jnp.maximum(one, -8.0 * SUN_COS)
    straight = jnp.maximum(one + two, -8.0) + jnp.maximum(one - two, -8.0)
    return (straight * SUN_COS + (slanted + 32.0 * SUN_COS)) * scale


def chosen(index, options):
    value = options[0]
    for k, option in enumerate(options[1:], 1):
        value = jnp.where(index == k, option, value)
    return value


def pooled(both, pool):
    high = both.astype(jnp.bfloat16)
    low = (both - high.astype(jnp.float32)).astype(jnp.bfloat16)
    return jnp.dot(high, pool, preferred_element_type=jnp.float32) + jnp.dot(
        low, pool, preferred_element_type=jnp.float32
    )


def got_col(m, parity):
    return (TC_DEV - 1 - m) + parity * (2 * m - (TC_DEV - 1))


def render(row_weights, source, col_weights):
    inner_rows = jnp.dot(row_weights, source, preferred_element_type=jnp.float32).astype(jnp.bfloat16)
    return jnp.dot(inner_rows, col_weights, preferred_element_type=jnp.float32)


def row_pairs(ref, where, count):
    return ref[(*where, pl.ds(0, count, stride=2), slice(None))] + ref[(*where, pl.ds(1, count, stride=2), slice(None))]


def pooling_matrix():
    rows = lax.broadcasted_iota(jnp.int32, (B, HALF), 0)
    cols = lax.broadcasted_iota(jnp.int32, (B, HALF), 1)
    return jnp.where(rows // 2 == cols, 0.25, 0.0).astype(jnp.bfloat16)


def kernel(
    n_row, n_col,
    srow_hbm, ask_hbm, elev_hbm, roww_hbm, colw_hbm,
    merc_out, one_out, two_out, two_got, late_out,
    srow_ref, sblock_ref, padded, shaded, asked_s, sendbuf, merged, roww, colw, tiles, ones, two_own, two_send, late_source,
    *rest,
):
    recv = rest[:16]
    (load_sem, ask_send, ask_recv, ask_local, halo_send, halo_recv,
     strip_send, strip_recv, two_sems, out_sem) = rest[16:]
    row = lax.axis_index("row")
    col = lax.axis_index("col")
    rows, cols = elev_hbm.shape
    parity = lax.rem(row, 2)
    up = lax.rem(row + n_row - 1, n_row)
    down = lax.rem(row + 1, n_row)
    left = lax.rem(col + n_col - 1, n_col)
    right = lax.rem(col + 1, n_col)
    last = TC_DEV - 1

    def sent_col(m):
        return m + parity * (last - 2 * m)

    def load_block(m):
        lane = pl.multiple_of(sent_col(m) * B, B)
        return pltpu.make_async_copy(
            elev_hbm.at[:, pl.ds(lane, B)],
            padded.at[pl.ds(PAD_R, rows), pl.ds(lane + PAD_C, B)],
            load_sem.at[m],
        )

    loads = {m: load_block(m) for m in (1, 0, 2, 3, 4, 5, 6, 7)}
    for copy in loads.values():
        copy.start()

    numbers = [
        pltpu.make_async_copy(srow_hbm, srow_ref, ask_local.at[1]),
        pltpu.make_async_copy(ask_hbm, sblock_ref, ask_local.at[2]),
    ]
    for copy in numbers:
        copy.start()

    around = [(up, col), (down, col), (row, left), (row, right)]
    barrier = pltpu.get_barrier_semaphore()
    for device in around:
        pl.semaphore_signal(barrier, inc=1, device_id=device, device_id_type=MESH)
    pl.semaphore_wait(barrier, len(around))

    def remote(src, dst, send_sem, recv_sem, device):
        return pltpu.make_async_remote_copy(
            src_ref=src, dst_ref=dst, send_sem=send_sem, recv_sem=recv_sem, device_id=device, device_id_type=MESH
        )

    asks = [
        remote(ask_hbm, asked_s.at[1], ask_send.at[0], ask_recv.at[1], (up, col)),
        remote(ask_hbm, asked_s.at[0], ask_send.at[1], ask_recv.at[0], (down, col)),
    ]
    for copy in asks:
        copy.start()

    top, bottom = pl.ds(0, PAD_R), pl.ds(PAD_R + rows, PAD_R)
    mid_c = pl.ds(PAD_C, cols)
    west, east = pl.ds(0, PAD_C), pl.ds(PAD_C + cols, PAD_C)
    first_r, last_r = pl.ds(0, PAD_R), pl.ds(rows - PAD_R, PAD_R)
    all_c = pl.ds(0, cols)
    halos = [
        remote(elev_hbm.at[first_r, all_c], padded.at[bottom, mid_c], halo_send.at[0], halo_recv.at[0], (up, col)),
        remote(elev_hbm.at[last_r, all_c], padded.at[top, mid_c], halo_send.at[1], halo_recv.at[1], (down, col)),
    ]
    for copy in halos:
        copy.start()
    every_r = pl.ds(0, rows + 2 * PAD_R)
    inner_west, inner_east = pl.ds(PAD_C, PAD_C), pl.ds(cols, PAD_C)
    sides = [
        remote(padded.at[every_r, inner_west], padded.at[every_r, east], halo_send.at[2], halo_recv.at[2], (row, left)),
        remote(padded.at[every_r, inner_east], padded.at[every_r, west], halo_send.at[3], halo_recv.at[3], (row, right)),
    ]
    load_roww = pltpu.make_async_copy(roww_hbm, roww, load_sem.at[TC_DEV])
    load_colw = pltpu.make_async_copy(colw_hbm, colw, load_sem.at[TC_DEV + 1])
    load_roww.start()
    load_colw.start()

    def clear(where):
        shape = tuple(s.size for s in where)
        padded[where] = jnp.zeros(shape, jnp.float32)

    def first_halo():
        for copy in asks:
            copy.wait_recv()
        halos[0].wait_recv()
        halos[1].wait_recv()

        @pl.when(row == 0)
        def _():
            clear((top, mid_c))

        @pl.when(row == n_row - 1)
        def _():
            clear((bottom, mid_c))

        for copy in numbers:
            copy.wait()

    arrived = set()

    pool = pooling_matrix()
    strips = []
    for step, m in enumerate(ORDER):
        if step == 2:
            for k in (0, last):
                if k not in arrived:
                    loads[k].wait()
                    arrived.add(k)
            for copy in sides:
                copy.start()
        if step == 4:
            for copy in sides:
                copy.wait_recv()

            @pl.when(col == 0)
            def _():
                clear((every_r, west))

            @pl.when(col == n_col - 1)
            def _():
                clear((every_r, east))

        lane = pl.multiple_of(sent_col(m) * B, PAD_C)
        slot = step % 2

        def shade_band(i, carry, lane=lane, slot=slot):
            start = pl.multiple_of(i * BAND, BAND)
            cells = padded[pl.ds(start, BAND + 2 * PAD_R), pl.ds(lane, B + 2 * PAD_C)]
            shaded[slot, pl.ds(start, BAND), :] = shade(cells, BAND).astype(jnp.bfloat16)
            return carry

        for k in (m - 1, m, m + 1):
            if 0 <= k <= last and k not in arrived:
                loads[k].wait()
                arrived.add(k)
        bands = rows // BAND
        if step == 0:
            lax.fori_loop(1, bands - 1, shade_band, 0, unroll=2)
            first_halo()
            lax.fori_loop(0, 2, lambda i, c: shade_band(i * (bands - 1), c), 0)
        else:
            lax.fori_loop(0, bands, shade_band, 0, unroll=2)
        for g in range(TR_DEV):
            for side in range(2):
                sendbuf[side, m, g] = chosen(
                    lax.div(asked_s[side, 0, g * TC_DEV], TC_DEV),
                    [shaded[slot, k * B : (k + 1) * B, :] for k in range(rows // B)],
                )
        for g in range(TR_DEV):
            for side, (device, place) in enumerate((((up, col), 2), ((down, col), 0))):
                copy = remote(
                    sendbuf.at[side, m, g],
                    recv[m * TR_DEV + g].at[place],
                    strip_send.at[side, m, g],
                    strip_recv.at[side, m, g],
                    device,
                )
                copy.start()
                strips.append(((step, g, side), copy))
        for g in range(TR_DEV):
            recv[(last - m) * TR_DEV + g][1] = chosen(
                lax.div(sblock_ref[0, g * TC_DEV], TC_DEV),
                [shaded[slot, k * B : (k + 1) * B, :] for k in range(rows // B)],
            )
    strips = dict(strips)

    load_roww.wait()
    load_colw.wait()
    outs = []
    two_copy = remote(two_send, two_got, two_sems.at[0], two_sems.at[1], (row + 1 - 2 * parity, col))

    def out_copy(src, dst):
        copy = pltpu.make_async_copy(src, dst, out_sem.at[len(outs)])
        copy.start()
        outs.append(copy)

    def make_target(g, m):
        j = got_col(m, parity)
        t = g * TC_DEV + j
        place = g * TC_DEV + m
        near = [k for k in (m - 1, m, m + 1) if 0 <= k <= last]
        wanted = lax.rem(sblock_ref[0, t], TC_DEV)
        where = wanted + (1 - parity) * (last - 2 * wanted)
        source = chosen(where - near[0], [merged[g, k] for k in near])
        if (g, m) in LATE:
            spot = LATE.index((g, m))
            late_source[spot] = source
            out_copy(late_source.at[spot], late_out.at[0, spot])
            return
        tile = render(roww[t], source, colw[t])
        sums = []
        for half in range(2):
            tiles[place, half] = tile[:, half * HALF : (half + 1) * HALF]
            lane = pl.multiple_of(j * B + half * HALF, HALF)
            out_copy(tiles.at[place, half], merc_out.at[pl.ds(g * B, B), pl.ds(lane, HALF)])
            sums.append(row_pairs(tiles, (place, half), HALF))
        where = (g * 4 + m // 2, lax.rem(j, 2))
        ones[where] = pooled(jnp.concatenate(sums, axis=1), pool)
        lane = pl.multiple_of(j * HALF, HALF)
        out_copy(ones.at[where], one_out.at[pl.ds(g * HALF, HALF), pl.ds(lane, HALF)])

    def make_coarse(g, pair):
        actual = lax.div(got_col(2 * pair, parity), 2)
        lane = pl.multiple_of(lax.rem(actual, 2) * HALF, HALF)
        sums = [row_pairs(ones, (g * 4 + pair, half), QUARTER) for half in range(2)]
        block = pooled(jnp.concatenate(sums, axis=1), pool)
        where = pl.ds(g * QUARTER, QUARTER), pl.ds(lane, HALF)
        if pair < 2:
            two_send[where] = block.astype(jnp.bfloat16)
        else:
            two_own[where] = block

    for spot, (g, m) in enumerate(LATE):
        t = g * TC_DEV + got_col(m, parity)
        out_copy(roww.at[t], late_out.at[1, spot])
        out_copy(colw.at[t], late_out.at[2, spot])

    done = set()
    for step, m in enumerate(ORDER):
        for g in range(TR_DEV):
            strips[step, g, 0].wait_recv()
            strips[step, g, 1].wait_recv()
            side = srow_ref[0, g * TC_DEV] - row + 1
            merged[g, m] = chosen(side, [recv[m * TR_DEV + g][k] for k in range(3)])
            for target in READY[step]:
                make_target(g, target)
                done.add((g, target))
                pair = target // 2
                both = (g, 2 * pair), (g, 2 * pair + 1)
                if all(x in done and x not in LATE for x in both):
                    make_coarse(g, pair)
        if step == 4:
            two_copy.start()
    out_copy(two_own, two_out)
    two_copy.wait_recv()
    for copy in outs:
        copy.wait()
    two_copy.wait_send()
    for copy in asks + halos + sides + list(strips.values()):
        copy.wait_send()


def finish(merc_in, one_in, two_in, two_got, late, merc_hbm, one_hbm, two_hbm, tiles, ones, coarse, other, sem):
    parity = lax.rem(lax.axis_index("row"), 2)
    copies = []

    def start(src, dst):
        copy = pltpu.make_async_copy(src, dst, sem.at[len(copies)])
        copy.start()
        copies.append(copy)

    def same(src, dst, rows, cols):
        start(src.at[rows, cols], dst.at[rows, cols])

    width = TC_DEV * B
    most = 6 * B
    same(merc_in, merc_hbm, pl.ds(0, B), pl.ds(0, width))
    same(merc_in, merc_hbm, pl.ds(B, B), pl.ds(pl.multiple_of((1 - parity) * (width - most), B), most))
    same(one_in, one_hbm, pl.ds(0, HALF), pl.ds(0, width // 2))
    same(one_in, one_hbm, pl.ds(HALF, HALF), pl.ds(pl.multiple_of((1 - parity) * (width - most) // 2, HALF), most // 2))
    own = parity * HALF
    start(two_in.at[pl.ds(0, QUARTER), :], two_hbm.at[pl.ds(pl.multiple_of(own, QUARTER), QUARTER), :])
    low = pl.ds(pl.multiple_of(own + QUARTER, QUARTER), QUARTER)
    lane = pl.ds(pl.multiple_of((1 - parity) * HALF, HALF), HALF)
    start(two_in.at[pl.ds(QUARTER, QUARTER), lane], two_hbm.at[low, lane])
    other[...] = two_got[...].astype(jnp.float32)
    start(other, two_hbm.at[pl.ds(pl.multiple_of((1 - parity) * HALF, HALF), HALF), :])

    pool = pooling_matrix()
    for spot, (g, m) in enumerate(LATE):
        j = got_col(m, parity)
        tile = render(late[1, spot], late[0, spot], late[2, spot])
        sums = []
        for half in range(2):
            tiles[spot, half] = tile[:, half * HALF : (half + 1) * HALF]
            lane = pl.multiple_of(j * B + half * HALF, HALF)
            start(tiles.at[spot, half], merc_hbm.at[pl.ds(g * B, B), pl.ds(lane, HALF)])
            sums.append(row_pairs(tiles, (spot, half), HALF))
        ones[lax.rem(j, 2)] = pooled(jnp.concatenate(sums, axis=1), pool)
        start(ones.at[lax.rem(j, 2)], one_hbm.at[pl.ds(g * HALF, HALF), pl.ds(pl.multiple_of(j * HALF, HALF), HALF)])
    sums = [row_pairs(ones, (half,), QUARTER) for half in range(2)]
    coarse[...] = pooled(jnp.concatenate(sums, axis=1), pool)
    start(coarse, two_hbm.at[low, pl.ds(pl.multiple_of(parity * HALF, HALF), HALF)])
    for copy in copies:
        copy.wait()


def per_device(n_row, n_col, elevation, source_row, source_block, row_weights, col_weights):
    rows, cols = elevation.shape
    targets = source_row.shape[0]
    source_row = source_row.reshape(1, targets)
    source_block = source_block.reshape(1, targets)
    anywhere = pl.BlockSpec(memory_space=pl.ANY)
    in_hbm = pl.BlockSpec(memory_space=pltpu.HBM)
    operands = (source_row, source_block, elevation, row_weights, col_weights)
    vmem, bf16, f32 = pltpu.VMEM, jnp.bfloat16, jnp.float32
    dma = pltpu.SemaphoreType.DMA
    n_out = 3 * targets + 1
    images = (
        jax.ShapeDtypeStruct((TR_DEV * B, TC_DEV * B), f32),
        jax.ShapeDtypeStruct((TR_DEV * HALF, TC_DEV * HALF), f32),
        jax.ShapeDtypeStruct((B, B), f32),
    )
    parts = pl.pallas_call(
        functools.partial(kernel, n_row, n_col),
        out_shape=(
            *images[:2],
            jax.ShapeDtypeStruct((HALF, B), f32),
            jax.ShapeDtypeStruct((HALF, B), bf16),
            jax.ShapeDtypeStruct((3, len(LATE), B, B), bf16),
        ),
        in_specs=[in_hbm] * len(operands),
        out_specs=(anywhere,) * 5,
        scratch_shapes=[
            pltpu.SMEM((1, targets), jnp.int32),
            pltpu.SMEM((1, targets), jnp.int32),
            vmem((rows + 2 * PAD_R, cols + 2 * PAD_C), f32),
            vmem((2, rows, B), bf16),
            pltpu.SMEM((2, 1, targets), jnp.int32),
            vmem((2, TC_DEV, TR_DEV, B, B), bf16),
            vmem((TR_DEV, TC_DEV, B, B), bf16),
            vmem((targets, B, B), bf16),
            vmem((targets, B, B), bf16),
            vmem((targets, 2, B, HALF), f32),
            vmem((targets // 2, 2, HALF, HALF), f32),
            vmem((HALF, B), f32),
            vmem((HALF, B), bf16),
            vmem((len(LATE), B, B), bf16),
        ]
        + [vmem((3, B, B), bf16)] * targets
        + [
            dma((TC_DEV + 2,)), dma((2,)), dma((2,)), dma((3,)), dma((4,)), dma((4,)),
            dma((2, TC_DEV, TR_DEV)), dma((2, TC_DEV, TR_DEV)), dma((2,)), dma((n_out,)),
        ],
        compiler_params=pltpu.CompilerParams(
            collective_id=0, has_side_effects=True, vmem_limit_bytes=44 * 1024 * 1024
        ),
        name="hillshade_tiles",
    )(*(pltpu.with_memory_space_constraint(x, pltpu.HBM) for x in operands))
    mercator, one, two = pl.pallas_call(
        finish,
        out_shape=images,
        in_specs=[anywhere] * 3 + [pl.BlockSpec(memory_space=vmem)] * 2,
        out_specs=(in_hbm,) * 3,
        scratch_shapes=[
            vmem((len(LATE), 2, B, HALF), f32),
            vmem((2, HALF, HALF), f32),
            vmem((QUARTER, HALF), f32),
            vmem((HALF, B), f32),
            dma((7 + 3 * len(LATE) + 1,)),
        ],
        compiler_params=pltpu.CompilerParams(vmem_limit_bytes=8 * 1024 * 1024),
        name="hillshade_finish",
    )(*parts)
    return mercator, one, two.reshape(1, 1, B, B)


def solution(mesh):
    in_specs = (
        P("row", "col"),
        P(("row", "col"), None),
        P(("row", "col"), None),
        P(("row", "col"), None, None),
        P(("row", "col"), None, None),
    )
    out_specs = (P("row", "col"), P("row", "col"), P("row", "col", None, None))
    return jax.shard_map(
        functools.partial(per_device, mesh.shape["row"], mesh.shape["col"]),
        mesh=mesh, in_specs=in_specs, out_specs=out_specs, check_vma=False,
    )
```

```python
import functools
import math

import jax
import jax.numpy as jnp
from jax import lax
from jax.experimental import pallas as pl
from jax.experimental.pallas import tpu as pltpu
from jax.sharding import PartitionSpec as P

B = 256
HALF = B // 2
QUARTER = B // 4
TR_DEV = 2
TC_DEV = 8
PAD_R = 8
PAD_C = 128
BAND = 64
ORDER = (1, 2, 3, 4, 0, 5, 6, 7)
READY = ((), (), (2,), (3,), (0, 1), (4,), (5,), (6, 7))
LATE = ((1, 6), (1, 7))

SUN_COS = math.cos(math.pi / 4.0)
MESH = pl.DeviceIdType.MESH


def shade(cells, band):
    height, width = cells.shape
    beside = cells + pltpu.roll(cells, width - 1, 1)
    box = beside + pltpu.roll(beside, height - 1, 0)
    box_up = pltpu.roll(box, 1, 0)
    middle = slice(PAD_R, PAD_R + band), slice(PAD_C, width - PAD_C)
    one = box[middle] - pltpu.roll(box_up, 1, 1)[middle]
    two = box_up[middle] - pltpu.roll(box, 1, 1)[middle]
    scale = lax.rsqrt((one * one + two * two) * 32.0 + 1024.0)
    slanted = jnp.maximum(two, -8.0 * SUN_COS) + jnp.maximum(one, -8.0 * SUN_COS)
    straight = jnp.maximum(one + two, -8.0) + jnp.maximum(one - two, -8.0)
    return (straight * SUN_COS + (slanted + 32.0 * SUN_COS)) * scale


def chosen(index, options):
    value = options[0]
    for k, option in enumerate(options[1:], 1):
        value = jnp.where(index == k, option, value)
    return value


def pooled(both, pool):
    high = both.astype(jnp.bfloat16)
    low = (both - high.astype(jnp.float32)).astype(jnp.bfloat16)
    return jnp.dot(high, pool, preferred_element_type=jnp.float32) + jnp.dot(
        low, pool, preferred_element_type=jnp.float32
    )


def got_col(m, parity):
    return (TC_DEV - 1 - m) + parity * (2 * m - (TC_DEV - 1))


def render(row_weights, source, col_weights):
    inner_rows = jnp.dot(row_weights, source, preferred_element_type=jnp.float32).astype(jnp.bfloat16)
    return jnp.dot(inner_rows, col_weights, preferred_element_type=jnp.float32)


def row_pairs(ref, where, count):
    return ref[(*where, pl.ds(0, count, stride=2), slice(None))] + ref[(*where, pl.ds(1, count, stride=2), slice(None))]


def pooling_matrix():
    rows = lax.broadcasted_iota(jnp.int32, (B, HALF), 0)
    cols = lax.broadcasted_iota(jnp.int32, (B, HALF), 1)
    return jnp.where(rows // 2 == cols, 0.25, 0.0).astype(jnp.bfloat16)


def kernel(
    n_row, n_col,
    srow_hbm, ask_hbm, elev_hbm, roww_hbm, colw_hbm,
    merc_out, one_out, two_out, two_got, late_out,
    srow_ref, sblock_ref, padded, shaded, asked_s, sendbuf, merged, roww, colw, tiles, ones, two_own, two_send, late_source, blind_send, blind_got,
    *rest,
):
    recv = rest[:16]
    (first_sem, load_sem, early_send, early_recv, blind_sems, ask_send, ask_recv, ask_local, halo_send, halo_recv,
     strip_send, strip_recv, two_sems, out_sem) = rest[16:]
    row = lax.axis_index("row")
    col = lax.axis_index("col")
    rows, cols = elev_hbm.shape
    parity = lax.rem(row, 2)
    up = lax.rem(row + n_row - 1, n_row)
    down = lax.rem(row + 1, n_row)
    left = lax.rem(col + n_col - 1, n_col)
    right = lax.rem(col + 1, n_col)
    last = TC_DEV - 1

    def sent_col(m):
        return m + parity * (last - 2 * m)

    pieces = rows // B
    span = B + 2 * PAD_C
    first_lane = pl.multiple_of(sent_col(ORDER[0]) * B - PAD_C, PAD_C)
    narrow, wide = PAD_C, cols - span - PAD_C

    def load(row_start, height, lane, width, sem):
        return pltpu.make_async_copy(
            elev_hbm.at[pl.ds(row_start, height), pl.ds(lane, width)],
            padded.at[pl.ds(row_start + PAD_R, height), pl.ds(lane + PAD_C, width)],
            sem,
        )

    def first_load(i):
        return load(pl.multiple_of(i * B, B), B, first_lane, span, first_sem.at[i])

    for i in range(pieces):
        first_load(i).start()
    rest = [
        load(0, rows, pl.multiple_of((1 - parity) * (narrow + span), PAD_C), wide, load_sem.at[0]),
        load(0, rows, pl.multiple_of(parity * (cols - narrow), PAD_C), narrow, load_sem.at[1]),
        pltpu.make_async_copy(roww_hbm, roww, load_sem.at[2]),
        pltpu.make_async_copy(colw_hbm, colw, load_sem.at[3]),
    ]

    numbers = [
        pltpu.make_async_copy(srow_hbm, srow_ref, ask_local.at[0]),
        pltpu.make_async_copy(ask_hbm, sblock_ref, ask_local.at[1]),
    ]
    for copy in numbers:
        copy.start()

    around = [(up, col), (down, col), (row, left), (row, right)]
    barrier = pltpu.get_barrier_semaphore()
    for device in around:
        pl.semaphore_signal(barrier, inc=1, device_id=device, device_id_type=MESH)
    pl.semaphore_wait(barrier, len(around))

    def remote(src, dst, send_sem, recv_sem, device):
        return pltpu.make_async_remote_copy(
            src_ref=src, dst_ref=dst, send_sem=send_sem, recv_sem=recv_sem, device_id=device, device_id_type=MESH
        )

    asks = [
        remote(ask_hbm, asked_s.at[1], ask_send.at[0], ask_recv.at[1], (up, col)),
        remote(ask_hbm, asked_s.at[0], ask_send.at[1], ask_recv.at[0], (down, col)),
    ]
    for copy in asks:
        copy.start()

    top, bottom = pl.ds(0, PAD_R), pl.ds(PAD_R + rows, PAD_R)
    mid_c = pl.ds(PAD_C, cols)
    west, east = pl.ds(0, PAD_C), pl.ds(PAD_C + cols, PAD_C)
    first_r, last_r = pl.ds(0, PAD_R), pl.ds(rows - PAD_R, PAD_R)
    all_c = pl.ds(0, cols)
    halos = [
        remote(elev_hbm.at[first_r, all_c], padded.at[bottom, mid_c], halo_send.at[0], halo_recv.at[0], (up, col)),
        remote(elev_hbm.at[last_r, all_c], padded.at[top, mid_c], halo_send.at[1], halo_recv.at[1], (down, col)),
    ]
    for copy in halos:
        copy.start()
    every_r = pl.ds(0, rows + 2 * PAD_R)
    inner_west, inner_east = pl.ds(PAD_C, PAD_C), pl.ds(cols, PAD_C)
    sides = [
        remote(padded.at[every_r, inner_west], padded.at[every_r, east], halo_send.at[2], halo_recv.at[2], (row, left)),
        remote(padded.at[every_r, inner_east], padded.at[every_r, west], halo_send.at[3], halo_recv.at[3], (row, right)),
    ]
    def clear(where):
        shape = tuple(s.size for s in where)
        padded[where] = jnp.zeros(shape, jnp.float32)

    def first_halo():
        for copy in asks:
            copy.wait_recv()
        halos[0].wait_recv()
        halos[1].wait_recv()

        @pl.when(row == 0)
        def _():
            clear((top, mid_c))

        @pl.when(row == n_row - 1)
        def _():
            clear((bottom, mid_c))

        for copy in numbers:
            copy.wait()

    pool = pooling_matrix()
    bands = rows // BAND
    per_piece = B // BAND
    units = [(step, ORDER[step], half * HALF, HALF) for step in range(2) for half in range(2)]
    units += [(step, m, 0, B) for step, m in enumerate(ORDER) if step > 1]
    half_bands = HALF // BAND
    ahead = 3

    def half_band(i, half):
        return lax.div(i, half_bands) * per_piece + lax.rem(i, half_bands) + half * half_bands

    blind = []

    def send_blind(k):
        for side, (device, place) in enumerate((((up, col), 1), ((down, col), 0))):
            copy = remote(
                blind_send.at[k], blind_got.at[place, k], blind_sems.at[0, side, k], blind_sems.at[1, side, k], device
            )
            copy.start()
            blind.append(copy)

    strips = []
    for unit, (step, m, offset, height) in enumerate(units):
        if unit == 4:
            for copy in sides:
                copy.start()
        if step == 4:
            for copy in sides:
                copy.wait_recv()

            @pl.when(col == 0)
            def _():
                clear((every_r, west))

            @pl.when(col == n_col - 1)
            def _():
                clear((every_r, east))

        lane = pl.multiple_of(sent_col(m) * B, PAD_C)
        slot = step % 2

        def shade_band(i, carry, lane=lane, slot=slot):
            start = pl.multiple_of(i * BAND, BAND)
            cells = padded[pl.ds(start, BAND + 2 * PAD_R), pl.ds(lane, B + 2 * PAD_C)]
            shaded[slot, pl.ds(start, BAND), :] = shade(cells, BAND).astype(jnp.bfloat16)
            return carry

        def first_half(i, carry, shade_band=shade_band):
            return shade_band(half_band(i, 0), carry)

        def second_half(i, carry, shade_band=shade_band):
            return shade_band(half_band(i, 1), carry)

        sent = slice(offset, offset + height)
        if unit == 0:
            for k in range(pieces):
                first_load(k).wait()
                shade_band(k * per_piece + 1, 0)
                rows_k = slice(k * B + BAND, k * B + 2 * BAND)
                blind_send[k] = shaded[slot, rows_k, :]
                if k > 0:
                    send_blind(k - 1)
            for copy in rest:
                copy.start()
            lax.fori_loop(1, pieces, lambda k, c: shade_band(k * per_piece, c), 0)
            send_blind(pieces - 1)
            lax.fori_loop(0, ahead, second_half, 0)
            first_halo()
            shade_band(0, 0)
            sent = slice(0, BAND)
        elif unit == 1:
            lax.fori_loop(ahead, pieces * half_bands, second_half, 0)
        elif unit == 2:
            rest[0].wait()
            rest[1].wait()
            lax.fori_loop(0, pieces * half_bands, first_half, 0, unroll=2)
        elif unit == 3:
            lax.fori_loop(0, pieces * half_bands, second_half, 0, unroll=2)
        else:
            lax.fori_loop(0, bands, shade_band, 0, unroll=2)
        part = slice(offset, offset + height)
        blocks = [slice(k * B + offset, k * B + offset + height) for k in range(pieces)]
        asked_rows = [slice(k * B + sent.start, k * B + sent.stop) for k in range(pieces)]
        for g in range(TR_DEV):
            for side in range(2):
                sendbuf[side, m, g, sent, :] = chosen(
                    lax.div(asked_s[side, 0, g * TC_DEV], TC_DEV), [shaded[slot, k, :] for k in asked_rows]
                )
        for g in range(TR_DEV):
            for side, (device, place) in enumerate((((up, col), 2), ((down, col), 0))):
                sems = (strip_send.at[side, m, g], strip_recv.at[side, m, g])
                if step < 2 and offset == 0:
                    sems = (early_send.at[side, step, g], early_recv.at[side, step, g])
                copy = remote(
                    sendbuf.at[side, m, g, sent, :],
                    recv[m * TR_DEV + g].at[place, sent, :],
                    *sems,
                    device,
                )
                copy.start()
                strips.append(((step, g), copy))
        for g in range(TR_DEV):
            recv[(last - m) * TR_DEV + g][1, part, :] = chosen(
                lax.div(sblock_ref[0, g * TC_DEV], TC_DEV), [shaded[slot, k, :] for k in blocks]
            )
    rest[2].wait()
    rest[3].wait()
    outs = []
    two_copy = remote(two_send, two_got, two_sems.at[0], two_sems.at[1], (row + 1 - 2 * parity, col))

    def out_copy(src, dst):
        copy = pltpu.make_async_copy(src, dst, out_sem.at[len(outs)])
        copy.start()
        outs.append(copy)

    def make_target(g, m):
        j = got_col(m, parity)
        t = g * TC_DEV + j
        place = g * TC_DEV + m
        near = [k for k in (m - 1, m, m + 1) if 0 <= k <= last]
        wanted = lax.rem(sblock_ref[0, t], TC_DEV)
        where = wanted + (1 - parity) * (last - 2 * wanted)
        source = chosen(where - near[0], [merged[g, k] for k in near])
        if (g, m) in LATE:
            spot = LATE.index((g, m))
            late_source[spot] = source
            out_copy(late_source.at[spot], late_out.at[0, spot])
            return
        tile = render(roww[t], source, colw[t])
        sums = []
        for half in range(2):
            tiles[place, half] = tile[:, half * HALF : (half + 1) * HALF]
            lane = pl.multiple_of(j * B + half * HALF, HALF)
            out_copy(tiles.at[place, half], merc_out.at[pl.ds(g * B, B), pl.ds(lane, HALF)])
            sums.append(row_pairs(tiles, (place, half), HALF))
        where = (g * 4 + m // 2, lax.rem(j, 2))
        ones[where] = pooled(jnp.concatenate(sums, axis=1), pool)
        lane = pl.multiple_of(j * HALF, HALF)
        out_copy(ones.at[where], one_out.at[pl.ds(g * HALF, HALF), pl.ds(lane, HALF)])

    def make_coarse(g, pair):
        actual = lax.div(got_col(2 * pair, parity), 2)
        lane = pl.multiple_of(lax.rem(actual, 2) * HALF, HALF)
        sums = [row_pairs(ones, (g * 4 + pair, half), QUARTER) for half in range(2)]
        block = pooled(jnp.concatenate(sums, axis=1), pool)
        where = pl.ds(g * QUARTER, QUARTER), pl.ds(lane, HALF)
        if pair < 2:
            two_send[where] = block.astype(jnp.bfloat16)
        else:
            two_own[where] = block

    for spot, (g, m) in enumerate(LATE):
        t = g * TC_DEV + got_col(m, parity)
        out_copy(roww.at[t], late_out.at[1, spot])
        out_copy(colw.at[t], late_out.at[2, spot])

    done = set()
    for step, m in enumerate(ORDER):
        for g in range(TR_DEV):
            for key, copy in strips:
                if key == (step, g):
                    copy.wait_recv()
            side = srow_ref[0, g * TC_DEV] - row + 1
            if step == 0:
                if g == 0:
                    for copy in blind:
                        copy.wait_recv()
                block = lax.div(sblock_ref[0, g * TC_DEV], TC_DEV)
                rows_b = slice(BAND, 2 * BAND)
                from_up, from_down = (chosen(block, [blind_got[p, k] for k in range(pieces)]) for p in range(2))
                merged[g, m, rows_b, :] = chosen(side, [from_up, recv[m * TR_DEV + g][1, rows_b, :], from_down])
                for rows_b in (slice(0, BAND), slice(2 * BAND, B)):
                    merged[g, m, rows_b, :] = chosen(side, [recv[m * TR_DEV + g][k, rows_b, :] for k in range(3)])
            else:
                merged[g, m] = chosen(side, [recv[m * TR_DEV + g][k] for k in range(3)])
            for target in READY[step]:
                make_target(g, target)
                done.add((g, target))
                pair = target // 2
                both = (g, 2 * pair), (g, 2 * pair + 1)
                if all(x in done and x not in LATE for x in both):
                    make_coarse(g, pair)
        if step == 4:
            two_copy.start()
    out_copy(two_own, two_out)
    two_copy.wait_recv()
    for copy in outs:
        copy.wait()
    two_copy.wait_send()
    for copy in asks + halos + sides + blind + [copy for _, copy in strips]:
        copy.wait_send()


def finish(merc_in, one_in, two_in, two_got, late, merc_hbm, one_hbm, two_hbm, tiles, ones, coarse, other, sem):
    parity = lax.rem(lax.axis_index("row"), 2)
    copies = []

    def start(src, dst):
        copy = pltpu.make_async_copy(src, dst, sem.at[len(copies)])
        copy.start()
        copies.append(copy)

    def same(src, dst, rows, cols):
        start(src.at[rows, cols], dst.at[rows, cols])

    width = TC_DEV * B
    most = 6 * B
    same(merc_in, merc_hbm, pl.ds(0, B), pl.ds(0, width))
    same(merc_in, merc_hbm, pl.ds(B, B), pl.ds(pl.multiple_of((1 - parity) * (width - most), B), most))
    same(one_in, one_hbm, pl.ds(0, HALF), pl.ds(0, width // 2))
    same(one_in, one_hbm, pl.ds(HALF, HALF), pl.ds(pl.multiple_of((1 - parity) * (width - most) // 2, HALF), most // 2))
    own = parity * HALF
    start(two_in.at[pl.ds(0, QUARTER), :], two_hbm.at[pl.ds(pl.multiple_of(own, QUARTER), QUARTER), :])
    low = pl.ds(pl.multiple_of(own + QUARTER, QUARTER), QUARTER)
    lane = pl.ds(pl.multiple_of((1 - parity) * HALF, HALF), HALF)
    start(two_in.at[pl.ds(QUARTER, QUARTER), lane], two_hbm.at[low, lane])
    other[...] = two_got[...].astype(jnp.float32)
    start(other, two_hbm.at[pl.ds(pl.multiple_of((1 - parity) * HALF, HALF), HALF), :])

    pool = pooling_matrix()
    for spot, (g, m) in enumerate(LATE):
        j = got_col(m, parity)
        tile = render(late[1, spot], late[0, spot], late[2, spot])
        sums = []
        for half in range(2):
            tiles[spot, half] = tile[:, half * HALF : (half + 1) * HALF]
            lane = pl.multiple_of(j * B + half * HALF, HALF)
            start(tiles.at[spot, half], merc_hbm.at[pl.ds(g * B, B), pl.ds(lane, HALF)])
            sums.append(row_pairs(tiles, (spot, half), HALF))
        ones[lax.rem(j, 2)] = pooled(jnp.concatenate(sums, axis=1), pool)
        start(ones.at[lax.rem(j, 2)], one_hbm.at[pl.ds(g * HALF, HALF), pl.ds(pl.multiple_of(j * HALF, HALF), HALF)])
    sums = [row_pairs(ones, (half,), QUARTER) for half in range(2)]
    coarse[...] = pooled(jnp.concatenate(sums, axis=1), pool)
    start(coarse, two_hbm.at[low, pl.ds(pl.multiple_of(parity * HALF, HALF), HALF)])
    for copy in copies:
        copy.wait()


def per_device(n_row, n_col, elevation, source_row, source_block, row_weights, col_weights):
    rows, cols = elevation.shape
    targets = source_row.shape[0]
    source_row = source_row.reshape(1, targets)
    source_block = source_block.reshape(1, targets)
    anywhere = pl.BlockSpec(memory_space=pl.ANY)
    in_hbm = pl.BlockSpec(memory_space=pltpu.HBM)
    operands = (source_row, source_block, elevation, row_weights, col_weights)
    vmem, bf16, f32 = pltpu.VMEM, jnp.bfloat16, jnp.float32
    dma = pltpu.SemaphoreType.DMA
    n_out = 3 * targets + 1
    images = (
        jax.ShapeDtypeStruct((TR_DEV * B, TC_DEV * B), f32),
        jax.ShapeDtypeStruct((TR_DEV * HALF, TC_DEV * HALF), f32),
        jax.ShapeDtypeStruct((B, B), f32),
    )
    parts = pl.pallas_call(
        functools.partial(kernel, n_row, n_col),
        out_shape=(
            *images[:2],
            jax.ShapeDtypeStruct((HALF, B), f32),
            jax.ShapeDtypeStruct((HALF, B), bf16),
            jax.ShapeDtypeStruct((3, len(LATE), B, B), bf16),
        ),
        in_specs=[in_hbm] * len(operands),
        out_specs=(anywhere,) * 5,
        scratch_shapes=[
            pltpu.SMEM((1, targets), jnp.int32),
            pltpu.SMEM((1, targets), jnp.int32),
            vmem((rows + 2 * PAD_R, cols + 2 * PAD_C), f32),
            vmem((2, rows, B), bf16),
            pltpu.SMEM((2, 1, targets), jnp.int32),
            vmem((2, TC_DEV, TR_DEV, B, B), bf16),
            vmem((TR_DEV, TC_DEV, B, B), bf16),
            vmem((targets, B, B), bf16),
            vmem((targets, B, B), bf16),
            vmem((targets, 2, B, HALF), f32),
            vmem((targets // 2, 2, HALF, HALF), f32),
            vmem((HALF, B), f32),
            vmem((HALF, B), bf16),
            vmem((len(LATE), B, B), bf16),
            vmem((rows // B, BAND, B), bf16),
            vmem((2, rows // B, BAND, B), bf16),
        ]
        + [vmem((3, B, B), bf16)] * targets
        + [
            dma((rows // B,)), dma((4,)), dma((2, 2, TR_DEV)), dma((2, 2, TR_DEV)),
            dma((2, 2, rows // B)), dma((2,)), dma((2,)), dma((2,)), dma((4,)), dma((4,)),
            dma((2, TC_DEV, TR_DEV)), dma((2, TC_DEV, TR_DEV)), dma((2,)), dma((n_out,)),
        ],
        compiler_params=pltpu.CompilerParams(
            collective_id=0, has_side_effects=True, vmem_limit_bytes=44 * 1024 * 1024
        ),
        name="hillshade_tiles",
    )(*(pltpu.with_memory_space_constraint(x, pltpu.HBM) for x in operands))
    mercator, one, two = pl.pallas_call(
        finish,
        out_shape=images,
        in_specs=[anywhere] * 3 + [pl.BlockSpec(memory_space=vmem)] * 2,
        out_specs=(in_hbm,) * 3,
        scratch_shapes=[
            vmem((len(LATE), 2, B, HALF), f32),
            vmem((2, HALF, HALF), f32),
            vmem((QUARTER, HALF), f32),
            vmem((HALF, B), f32),
            dma((7 + 3 * len(LATE) + 1,)),
        ],
        compiler_params=pltpu.CompilerParams(vmem_limit_bytes=8 * 1024 * 1024),
        name="hillshade_finish",
    )(*parts)
    return mercator, one, two.reshape(1, 1, B, B)


def solution(mesh):
    in_specs = (
        P("row", "col"),
        P(("row", "col"), None),
        P(("row", "col"), None),
        P(("row", "col"), None, None),
        P(("row", "col"), None, None),
    )
    out_specs = (P("row", "col"), P("row", "col"), P("row", "col", None, None))
    return jax.shard_map(
        functools.partial(per_device, mesh.shape["row"], mesh.shape["col"]),
        mesh=mesh, in_specs=in_specs, out_specs=out_specs, check_vma=False,
    )
```

```python
import functools
import math

import jax
import jax.numpy as jnp
from jax import lax
from jax.experimental import pallas as pl
from jax.experimental.pallas import tpu as pltpu
from jax.sharding import PartitionSpec as P

B = 256
HALF = B // 2
QUARTER = B // 4
TR_DEV = 2
TC_DEV = 8
PAD_R = 8
PAD_C = 128
BAND = 64
ORDER = (1, 2, 3, 4, 0, 5, 6, 7)
READY = ((), (), (2,), (3,), (0, 1), (4,), (5,), (6, 7))
LATE = ((1, 6), (1, 7))

SUN_COS = math.cos(math.pi / 4.0)
MESH = pl.DeviceIdType.MESH


def shade(cells, band):
    height, width = cells.shape
    beside = cells + pltpu.roll(cells, width - 1, 1)
    box = beside + pltpu.roll(beside, height - 1, 0)
    box_up = pltpu.roll(box, 1, 0)
    middle = slice(PAD_R, PAD_R + band), slice(PAD_C, width - PAD_C)
    one = box[middle] - pltpu.roll(box_up, 1, 1)[middle]
    two = box_up[middle] - pltpu.roll(box, 1, 1)[middle]
    scale = lax.rsqrt((one * one + two * two) * 32.0 + 1024.0)
    slanted = jnp.maximum(two, -8.0 * SUN_COS) + jnp.maximum(one, -8.0 * SUN_COS)
    straight = jnp.maximum(one + two, -8.0) + jnp.maximum(one - two, -8.0)
    return (straight * SUN_COS + (slanted + 32.0 * SUN_COS)) * scale


def chosen(index, options):
    value = options[0]
    for k, option in enumerate(options[1:], 1):
        value = jnp.where(index == k, option, value)
    return value


def pooled(both, pool):
    high = both.astype(jnp.bfloat16)
    low = (both - high.astype(jnp.float32)).astype(jnp.bfloat16)
    return jnp.dot(high, pool, preferred_element_type=jnp.float32) + jnp.dot(
        low, pool, preferred_element_type=jnp.float32
    )


def got_col(m, parity):
    return (TC_DEV - 1 - m) + parity * (2 * m - (TC_DEV - 1))


def render(row_weights, source, col_weights):
    inner_rows = jnp.dot(row_weights, source, preferred_element_type=jnp.float32).astype(jnp.bfloat16)
    return jnp.dot(inner_rows, col_weights, preferred_element_type=jnp.float32)


def row_pairs(ref, where, count):
    return ref[(*where, pl.ds(0, count, stride=2), slice(None))] + ref[(*where, pl.ds(1, count, stride=2), slice(None))]


def pooling_matrix():
    rows = lax.broadcasted_iota(jnp.int32, (B, HALF), 0)
    cols = lax.broadcasted_iota(jnp.int32, (B, HALF), 1)
    return jnp.where(rows // 2 == cols, 0.25, 0.0).astype(jnp.bfloat16)


def kernel(
    n_row, n_col,
    srow_hbm, ask_hbm, elev_hbm, roww_hbm, colw_hbm,
    merc_out, one_out, two_out, two_got, late_out,
    srow_ref, sblock_ref, padded, shaded, asked_s, sendbuf, merged, roww, colw, tiles, ones, two_own, two_send, late_source, blind_send, blind_got,
    *rest,
):
    recv = rest[:16]
    (first_sem, load_sem, early_send, early_recv, blind_sems, ask_send, ask_recv, ask_local, halo_send, halo_recv,
     strip_send, strip_recv, two_sems, out_sem) = rest[16:]
    row = lax.axis_index("row")
    col = lax.axis_index("col")
    rows, cols = elev_hbm.shape
    parity = lax.rem(row, 2)
    up = lax.rem(row + n_row - 1, n_row)
    down = lax.rem(row + 1, n_row)
    left = lax.rem(col + n_col - 1, n_col)
    right = lax.rem(col + 1, n_col)
    last = TC_DEV - 1

    def sent_col(m):
        return m + parity * (last - 2 * m)

    pieces = rows // B
    span = B + 2 * PAD_C
    first_lane = pl.multiple_of(sent_col(ORDER[0]) * B - PAD_C, PAD_C)
    narrow, wide = PAD_C, cols - span - PAD_C

    def load(row_start, height, lane, width, sem):
        return pltpu.make_async_copy(
            elev_hbm.at[pl.ds(row_start, height), pl.ds(lane, width)],
            padded.at[pl.ds(row_start + PAD_R, height), pl.ds(lane + PAD_C, width)],
            sem,
        )

    def first_load(i):
        return load(pl.multiple_of(i * B, B), B, first_lane, span, first_sem.at[i])

    for i in range(pieces):
        first_load(i).start()
    rest = [
        load(0, rows, pl.multiple_of((1 - parity) * (narrow + span), PAD_C), wide, load_sem.at[0]),
        load(0, rows, pl.multiple_of(parity * (cols - narrow), PAD_C), narrow, load_sem.at[1]),
        pltpu.make_async_copy(roww_hbm, roww, load_sem.at[2]),
        pltpu.make_async_copy(colw_hbm, colw, load_sem.at[3]),
    ]

    numbers = [
        pltpu.make_async_copy(srow_hbm, srow_ref, ask_local.at[0]),
        pltpu.make_async_copy(ask_hbm, sblock_ref, ask_local.at[1]),
    ]
    for copy in numbers:
        copy.start()

    around = [(up, col), (down, col), (row, left), (row, right)]
    barrier = pltpu.get_barrier_semaphore()
    for device in around:
        pl.semaphore_signal(barrier, inc=1, device_id=device, device_id_type=MESH)
    for copy in numbers:
        copy.wait()
    pl.semaphore_wait(barrier, len(around))

    def remote(src, dst, send_sem, recv_sem, device):
        return pltpu.make_async_remote_copy(
            src_ref=src, dst_ref=dst, send_sem=send_sem, recv_sem=recv_sem, device_id=device, device_id_type=MESH
        )

    asks = [
        remote(sblock_ref, asked_s.at[1], ask_send.at[0], ask_recv.at[1], (up, col)),
        remote(sblock_ref, asked_s.at[0], ask_send.at[1], ask_recv.at[0], (down, col)),
    ]
    for copy in asks:
        copy.start()

    top, bottom = pl.ds(0, PAD_R), pl.ds(PAD_R + rows, PAD_R)
    mid_c = pl.ds(PAD_C, cols)
    west, east = pl.ds(0, PAD_C), pl.ds(PAD_C + cols, PAD_C)
    first_r, last_r = pl.ds(0, PAD_R), pl.ds(rows - PAD_R, PAD_R)
    all_c = pl.ds(0, cols)
    halos = [
        remote(elev_hbm.at[first_r, all_c], padded.at[bottom, mid_c], halo_send.at[0], halo_recv.at[0], (up, col)),
        remote(elev_hbm.at[last_r, all_c], padded.at[top, mid_c], halo_send.at[1], halo_recv.at[1], (down, col)),
    ]
    for copy in halos:
        copy.start()
    every_r = pl.ds(0, rows + 2 * PAD_R)
    inner_west, inner_east = pl.ds(PAD_C, PAD_C), pl.ds(cols, PAD_C)
    sides = [
        remote(padded.at[every_r, inner_west], padded.at[every_r, east], halo_send.at[2], halo_recv.at[2], (row, left)),
        remote(padded.at[every_r, inner_east], padded.at[every_r, west], halo_send.at[3], halo_recv.at[3], (row, right)),
    ]
    def clear(where):
        shape = tuple(s.size for s in where)
        padded[where] = jnp.zeros(shape, jnp.float32)

    def first_halo():
        for copy in asks:
            copy.wait_recv()
        halos[0].wait_recv()
        halos[1].wait_recv()

        @pl.when(row == 0)
        def _():
            clear((top, mid_c))

        @pl.when(row == n_row - 1)
        def _():
            clear((bottom, mid_c))

    pool = pooling_matrix()
    bands = rows // BAND
    per_piece = B // BAND
    units = [(step, ORDER[step], half * HALF, HALF) for step in range(2) for half in range(2)]
    units += [(step, m, 0, B) for step, m in enumerate(ORDER) if step > 1]
    half_bands = HALF // BAND
    ahead = 6

    def half_band(i, half):
        return lax.div(i, half_bands) * per_piece + lax.rem(i, half_bands) + half * half_bands

    blind = []

    def send_blind(k):
        for side, (device, place) in enumerate((((up, col), 1), ((down, col), 0))):
            copy = remote(
                blind_send.at[k], blind_got.at[place, k], blind_sems.at[0, side, k], blind_sems.at[1, side, k], device
            )
            copy.start()
            blind.append(copy)

    strips = []
    for unit, (step, m, offset, height) in enumerate(units):
        if unit == 4:
            for copy in sides:
                copy.start()
        if step == 4:
            for copy in sides:
                copy.wait_recv()

            @pl.when(col == 0)
            def _():
                clear((every_r, west))

            @pl.when(col == n_col - 1)
            def _():
                clear((every_r, east))

        lane = pl.multiple_of(sent_col(m) * B, PAD_C)
        slot = step % 2

        def shade_band(i, carry, lane=lane, slot=slot):
            start = pl.multiple_of(i * BAND, BAND)
            cells = padded[pl.ds(start, BAND + 2 * PAD_R), pl.ds(lane, B + 2 * PAD_C)]
            shaded[slot, pl.ds(start, BAND), :] = shade(cells, BAND).astype(jnp.bfloat16)
            return carry

        def first_half(i, carry, shade_band=shade_band):
            return shade_band(half_band(i, 0), carry)

        def second_half(i, carry, shade_band=shade_band):
            return shade_band(half_band(i, 1), carry)

        sent = slice(offset, offset + height)
        if unit == 0:
            for k in range(pieces):
                first_load(k).wait()
                shade_band(k * per_piece + 1, 0)
                rows_k = slice(k * B + BAND, k * B + 2 * BAND)
                blind_send[k] = shaded[slot, rows_k, :]
                if k > 0:
                    send_blind(k - 1)
            for copy in rest:
                copy.start()
            lax.fori_loop(1, pieces, lambda k, c: shade_band(k * per_piece, c), 0)
            send_blind(pieces - 1)
            lax.fori_loop(0, ahead, second_half, 0)
            first_halo()
            shade_band(0, 0)
            sent = slice(0, BAND)
        elif unit == 1:
            lax.fori_loop(ahead, pieces * half_bands, second_half, 0)
        elif unit == 2:
            rest[0].wait()
            rest[1].wait()
            lax.fori_loop(0, pieces * half_bands, first_half, 0, unroll=2)
        elif unit == 3:
            lax.fori_loop(0, pieces * half_bands, second_half, 0, unroll=2)
        else:
            lax.fori_loop(0, bands, shade_band, 0, unroll=2)
        part = slice(offset, offset + height)
        blocks = [slice(k * B + offset, k * B + offset + height) for k in range(pieces)]
        asked_rows = [slice(k * B + sent.start, k * B + sent.stop) for k in range(pieces)]
        for g in range(TR_DEV):
            for side in range(2):
                sendbuf[side, m, g, sent, :] = chosen(
                    lax.div(asked_s[side, 0, g * TC_DEV], TC_DEV), [shaded[slot, k, :] for k in asked_rows]
                )
        for g in range(TR_DEV):
            for side, (device, place) in enumerate((((up, col), 2), ((down, col), 0))):
                sems = (strip_send.at[side, m, g], strip_recv.at[side, m, g])
                if step < 2 and offset == 0:
                    sems = (early_send.at[side, step, g], early_recv.at[side, step, g])
                copy = remote(
                    sendbuf.at[side, m, g, sent, :],
                    recv[m * TR_DEV + g].at[place, sent, :],
                    *sems,
                    device,
                )
                copy.start()
                strips.append(((step, g), copy))
        for g in range(TR_DEV):
            recv[(last - m) * TR_DEV + g][1, part, :] = chosen(
                lax.div(sblock_ref[0, g * TC_DEV], TC_DEV), [shaded[slot, k, :] for k in blocks]
            )
    rest[2].wait()
    rest[3].wait()
    outs = []
    two_copy = remote(two_send, two_got, two_sems.at[0], two_sems.at[1], (row + 1 - 2 * parity, col))

    def out_copy(src, dst):
        copy = pltpu.make_async_copy(src, dst, out_sem.at[len(outs)])
        copy.start()
        outs.append(copy)

    def make_target(g, m):
        j = got_col(m, parity)
        t = g * TC_DEV + j
        place = g * TC_DEV + m
        near = [k for k in (m - 1, m, m + 1) if 0 <= k <= last]
        wanted = lax.rem(sblock_ref[0, t], TC_DEV)
        where = wanted + (1 - parity) * (last - 2 * wanted)
        source = chosen(where - near[0], [merged[g, k] for k in near])
        if (g, m) in LATE:
            spot = LATE.index((g, m))
            late_source[spot] = source
            out_copy(late_source.at[spot], late_out.at[0, spot])
            return
        tile = render(roww[t], source, colw[t])
        sums = []
        for half in range(2):
            tiles[place, half] = tile[:, half * HALF : (half + 1) * HALF]
            lane = pl.multiple_of(j * B + half * HALF, HALF)
            out_copy(tiles.at[place, half], merc_out.at[pl.ds(g * B, B), pl.ds(lane, HALF)])
            sums.append(row_pairs(tiles, (place, half), HALF))
        where = (g * 4 + m // 2, lax.rem(j, 2))
        ones[where] = pooled(jnp.concatenate(sums, axis=1), pool)
        lane = pl.multiple_of(j * HALF, HALF)
        out_copy(ones.at[where], one_out.at[pl.ds(g * HALF, HALF), pl.ds(lane, HALF)])

    def make_coarse(g, pair):
        actual = lax.div(got_col(2 * pair, parity), 2)
        lane = pl.multiple_of(lax.rem(actual, 2) * HALF, HALF)
        sums = [row_pairs(ones, (g * 4 + pair, half), QUARTER) for half in range(2)]
        block = pooled(jnp.concatenate(sums, axis=1), pool)
        where = pl.ds(g * QUARTER, QUARTER), pl.ds(lane, HALF)
        if pair < 2:
            two_send[where] = block.astype(jnp.bfloat16)
        else:
            two_own[where] = block

    for spot, (g, m) in enumerate(LATE):
        t = g * TC_DEV + got_col(m, parity)
        out_copy(roww.at[t], late_out.at[1, spot])
        out_copy(colw.at[t], late_out.at[2, spot])

    done = set()
    for step, m in enumerate(ORDER):
        for g in range(TR_DEV):
            for key, copy in strips:
                if key == (step, g):
                    copy.wait_recv()
            side = srow_ref[0, g * TC_DEV] - row + 1
            if step == 0:
                if g == 0:
                    for copy in blind:
                        copy.wait_recv()
                block = lax.div(sblock_ref[0, g * TC_DEV], TC_DEV)
                rows_b = slice(BAND, 2 * BAND)
                from_up, from_down = (chosen(block, [blind_got[p, k] for k in range(pieces)]) for p in range(2))
                merged[g, m, rows_b, :] = chosen(side, [from_up, recv[m * TR_DEV + g][1, rows_b, :], from_down])
                for rows_b in (slice(0, BAND), slice(2 * BAND, B)):
                    merged[g, m, rows_b, :] = chosen(side, [recv[m * TR_DEV + g][k, rows_b, :] for k in range(3)])
            else:
                merged[g, m] = chosen(side, [recv[m * TR_DEV + g][k] for k in range(3)])
            for target in READY[step]:
                make_target(g, target)
                done.add((g, target))
                pair = target // 2
                both = (g, 2 * pair), (g, 2 * pair + 1)
                if all(x in done and x not in LATE for x in both):
                    make_coarse(g, pair)
        if step == 4:
            two_copy.start()
    out_copy(two_own, two_out)
    two_copy.wait_recv()
    for copy in outs:
        copy.wait()
    two_copy.wait_send()
    for copy in asks + halos + sides + blind + [copy for _, copy in strips]:
        copy.wait_send()


def finish(merc_in, one_in, two_in, two_got, late, merc_hbm, one_hbm, two_hbm, tiles, ones, coarse, other, sem):
    parity = lax.rem(lax.axis_index("row"), 2)
    copies = []

    def start(src, dst):
        copy = pltpu.make_async_copy(src, dst, sem.at[len(copies)])
        copy.start()
        copies.append(copy)

    def same(src, dst, rows, cols):
        start(src.at[rows, cols], dst.at[rows, cols])

    width = TC_DEV * B
    most = 6 * B
    same(merc_in, merc_hbm, pl.ds(0, B), pl.ds(0, width))
    same(merc_in, merc_hbm, pl.ds(B, B), pl.ds(pl.multiple_of((1 - parity) * (width - most), B), most))
    same(one_in, one_hbm, pl.ds(0, HALF), pl.ds(0, width // 2))
    same(one_in, one_hbm, pl.ds(HALF, HALF), pl.ds(pl.multiple_of((1 - parity) * (width - most) // 2, HALF), most // 2))
    own = parity * HALF
    start(two_in.at[pl.ds(0, QUARTER), :], two_hbm.at[pl.ds(pl.multiple_of(own, QUARTER), QUARTER), :])
    low = pl.ds(pl.multiple_of(own + QUARTER, QUARTER), QUARTER)
    lane = pl.ds(pl.multiple_of((1 - parity) * HALF, HALF), HALF)
    start(two_in.at[pl.ds(QUARTER, QUARTER), lane], two_hbm.at[low, lane])
    other[...] = two_got[...].astype(jnp.float32)
    start(other, two_hbm.at[pl.ds(pl.multiple_of((1 - parity) * HALF, HALF), HALF), :])

    pool = pooling_matrix()
    for spot, (g, m) in enumerate(LATE):
        j = got_col(m, parity)
        tile = render(late[1, spot], late[0, spot], late[2, spot])
        sums = []
        for half in range(2):
            tiles[spot, half] = tile[:, half * HALF : (half + 1) * HALF]
            lane = pl.multiple_of(j * B + half * HALF, HALF)
            start(tiles.at[spot, half], merc_hbm.at[pl.ds(g * B, B), pl.ds(lane, HALF)])
            sums.append(row_pairs(tiles, (spot, half), HALF))
        ones[lax.rem(j, 2)] = pooled(jnp.concatenate(sums, axis=1), pool)
        start(ones.at[lax.rem(j, 2)], one_hbm.at[pl.ds(g * HALF, HALF), pl.ds(pl.multiple_of(j * HALF, HALF), HALF)])
    sums = [row_pairs(ones, (half,), QUARTER) for half in range(2)]
    coarse[...] = pooled(jnp.concatenate(sums, axis=1), pool)
    start(coarse, two_hbm.at[low, pl.ds(pl.multiple_of(parity * HALF, HALF), HALF)])
    for copy in copies:
        copy.wait()


def per_device(n_row, n_col, elevation, source_row, source_block, row_weights, col_weights):
    rows, cols = elevation.shape
    targets = source_row.shape[0]
    source_row = source_row.reshape(1, targets)
    source_block = source_block.reshape(1, targets)
    anywhere = pl.BlockSpec(memory_space=pl.ANY)
    in_hbm = pl.BlockSpec(memory_space=pltpu.HBM)
    operands = (source_row, source_block, elevation, row_weights, col_weights)
    vmem, bf16, f32 = pltpu.VMEM, jnp.bfloat16, jnp.float32
    dma = pltpu.SemaphoreType.DMA
    n_out = 3 * targets + 1
    images = (
        jax.ShapeDtypeStruct((TR_DEV * B, TC_DEV * B), f32),
        jax.ShapeDtypeStruct((TR_DEV * HALF, TC_DEV * HALF), f32),
        jax.ShapeDtypeStruct((B, B), f32),
    )
    parts = pl.pallas_call(
        functools.partial(kernel, n_row, n_col),
        out_shape=(
            *images[:2],
            jax.ShapeDtypeStruct((HALF, B), f32),
            jax.ShapeDtypeStruct((HALF, B), bf16),
            jax.ShapeDtypeStruct((3, len(LATE), B, B), bf16),
        ),
        in_specs=[in_hbm] * len(operands),
        out_specs=(anywhere,) * 5,
        scratch_shapes=[
            pltpu.SMEM((1, targets), jnp.int32),
            pltpu.SMEM((1, targets), jnp.int32),
            vmem((rows + 2 * PAD_R, cols + 2 * PAD_C), f32),
            vmem((2, rows, B), bf16),
            pltpu.SMEM((2, 1, targets), jnp.int32),
            vmem((2, TC_DEV, TR_DEV, B, B), bf16),
            vmem((TR_DEV, TC_DEV, B, B), bf16),
            vmem((targets, B, B), bf16),
            vmem((targets, B, B), bf16),
            vmem((targets, 2, B, HALF), f32),
            vmem((targets // 2, 2, HALF, HALF), f32),
            vmem((HALF, B), f32),
            vmem((HALF, B), bf16),
            vmem((len(LATE), B, B), bf16),
            vmem((rows // B, BAND, B), bf16),
            vmem((2, rows // B, BAND, B), bf16),
        ]
        + [vmem((3, B, B), bf16)] * targets
        + [
            dma((rows // B,)), dma((4,)), dma((2, 2, TR_DEV)), dma((2, 2, TR_DEV)),
            dma((2, 2, rows // B)), dma((2,)), dma((2,)), dma((2,)), dma((4,)), dma((4,)),
            dma((2, TC_DEV, TR_DEV)), dma((2, TC_DEV, TR_DEV)), dma((2,)), dma((n_out,)),
        ],
        compiler_params=pltpu.CompilerParams(
            collective_id=0, has_side_effects=True, vmem_limit_bytes=44 * 1024 * 1024
        ),
        name="hillshade_tiles",
    )(*(pltpu.with_memory_space_constraint(x, pltpu.HBM) for x in operands))
    mercator, one, two = pl.pallas_call(
        finish,
        out_shape=images,
        in_specs=[anywhere] * 3 + [pl.BlockSpec(memory_space=vmem)] * 2,
        out_specs=(in_hbm,) * 3,
        scratch_shapes=[
            vmem((len(LATE), 2, B, HALF), f32),
            vmem((2, HALF, HALF), f32),
            vmem((QUARTER, HALF), f32),
            vmem((HALF, B), f32),
            dma((7 + 3 * len(LATE) + 1,)),
        ],
        compiler_params=pltpu.CompilerParams(vmem_limit_bytes=8 * 1024 * 1024),
        name="hillshade_finish",
    )(*parts)
    return mercator, one, two.reshape(1, 1, B, B)


def solution(mesh):
    in_specs = (
        P("row", "col"),
        P(("row", "col"), None),
        P(("row", "col"), None),
        P(("row", "col"), None, None),
        P(("row", "col"), None, None),
    )
    out_specs = (P("row", "col"), P("row", "col"), P("row", "col", None, None))
    return jax.shard_map(
        functools.partial(per_device, mesh.shape["row"], mesh.shape["col"]),
        mesh=mesh, in_specs=in_specs, out_specs=out_specs, check_vma=False,
    )
```

```python
import functools
import math

import jax
import jax.numpy as jnp
from jax import lax
from jax.experimental import pallas as pl
from jax.experimental.pallas import tpu as pltpu
from jax.sharding import PartitionSpec as P

B = 256
HALF = B // 2
QUARTER = B // 4
TR_DEV = 2
TC_DEV = 8
PAD_R = 8
PAD_C = 128
BAND = 64
ORDER = (1, 2, 3, 4, 0, 5, 6, 7)
READY = ((), (), (2,), (3,), (0, 1), (4,), (5,), (6, 7))
LATE = ((1, 6), (1, 7))

SUN_COS = math.cos(math.pi / 4.0)
MESH = pl.DeviceIdType.MESH


def shade(cells, band):
    height, width = cells.shape
    beside = cells + pltpu.roll(cells, width - 1, 1)
    box = beside + pltpu.roll(beside, height - 1, 0)
    box_up = pltpu.roll(box, 1, 0)
    middle = slice(PAD_R, PAD_R + band), slice(PAD_C, width - PAD_C)
    one = box[middle] - pltpu.roll(box_up, 1, 1)[middle]
    two = box_up[middle] - pltpu.roll(box, 1, 1)[middle]
    scale = lax.rsqrt((one * one + two * two) * 32.0 + 1024.0)
    slanted = jnp.maximum(two, -8.0 * SUN_COS) + jnp.maximum(one, -8.0 * SUN_COS)
    straight = jnp.maximum(one + two, -8.0) + jnp.maximum(one - two, -8.0)
    return (straight * SUN_COS + (slanted + 32.0 * SUN_COS)) * scale


def chosen(index, options):
    value = options[0]
    for k, option in enumerate(options[1:], 1):
        value = jnp.where(index == k, option, value)
    return value


def pooled(both, pool):
    high = both.astype(jnp.bfloat16)
    low = (both - high.astype(jnp.float32)).astype(jnp.bfloat16)
    return jnp.dot(high, pool, preferred_element_type=jnp.float32) + jnp.dot(
        low, pool, preferred_element_type=jnp.float32
    )


def got_col(m, parity):
    return (TC_DEV - 1 - m) + parity * (2 * m - (TC_DEV - 1))


def render(row_weights, source, col_weights):
    inner_rows = jnp.dot(row_weights, source, preferred_element_type=jnp.float32).astype(jnp.bfloat16)
    return jnp.dot(inner_rows, col_weights, preferred_element_type=jnp.float32)


def row_pairs(ref, where, count):
    return ref[(*where, pl.ds(0, count, stride=2), slice(None))] + ref[(*where, pl.ds(1, count, stride=2), slice(None))]


def pooling_matrix():
    rows = lax.broadcasted_iota(jnp.int32, (B, HALF), 0)
    cols = lax.broadcasted_iota(jnp.int32, (B, HALF), 1)
    return jnp.where(rows // 2 == cols, 0.25, 0.0).astype(jnp.bfloat16)


def kernel(
    n_row, n_col,
    srow_hbm, ask_hbm, elev_hbm, roww_hbm, colw_hbm,
    merc_out, one_out, two_out, two_got, late_out,
    srow_ref, sblock_ref, padded, shaded, asked_s, sendbuf, merged, roww, colw, tiles, ones, two_own, two_send, late_source, blind_send, blind_got,
    *rest,
):
    recv = rest[:16]
    (first_sem, load_sem, early_send, early_recv, blind_sems, ask_send, ask_recv, ask_local, halo_send, halo_recv,
     strip_send, strip_recv, two_sems, out_sem) = rest[16:]
    row = lax.axis_index("row")
    col = lax.axis_index("col")
    rows, cols = elev_hbm.shape
    parity = lax.rem(row, 2)
    up = lax.rem(row + n_row - 1, n_row)
    down = lax.rem(row + 1, n_row)
    left = lax.rem(col + n_col - 1, n_col)
    right = lax.rem(col + 1, n_col)
    last = TC_DEV - 1

    def sent_col(m):
        return m + parity * (last - 2 * m)

    pieces = rows // B
    span = B + 2 * PAD_C
    first_lane = pl.multiple_of(sent_col(ORDER[0]) * B - PAD_C, PAD_C)
    narrow, wide = PAD_C, cols - span - PAD_C

    def load(row_start, height, lane, width, sem):
        return pltpu.make_async_copy(
            elev_hbm.at[pl.ds(row_start, height), pl.ds(lane, width)],
            padded.at[pl.ds(row_start + PAD_R, height), pl.ds(lane + PAD_C, width)],
            sem,
        )

    def first_load(i):
        return load(pl.multiple_of(i * B, B), B, first_lane, span, first_sem.at[i])

    for i in range(pieces):
        first_load(i).start()
    rest = [
        load(0, rows, pl.multiple_of((1 - parity) * (narrow + span), PAD_C), wide, load_sem.at[0]),
        load(0, rows, pl.multiple_of(parity * (cols - narrow), PAD_C), narrow, load_sem.at[1]),
        pltpu.make_async_copy(roww_hbm, roww, load_sem.at[2]),
        pltpu.make_async_copy(colw_hbm, colw, load_sem.at[3]),
    ]

    numbers = [
        pltpu.make_async_copy(srow_hbm, srow_ref, ask_local.at[0]),
        pltpu.make_async_copy(ask_hbm, sblock_ref, ask_local.at[1]),
    ]
    for copy in numbers:
        copy.start()

    around = [(up, col), (down, col), (row, left), (row, right)]
    barrier = pltpu.get_barrier_semaphore()
    for device in around:
        pl.semaphore_signal(barrier, inc=1, device_id=device, device_id_type=MESH)
    for copy in numbers:
        copy.wait()
    pl.semaphore_wait(barrier, len(around))

    def remote(src, dst, send_sem, recv_sem, device):
        return pltpu.make_async_remote_copy(
            src_ref=src, dst_ref=dst, send_sem=send_sem, recv_sem=recv_sem, device_id=device, device_id_type=MESH
        )

    asks = [
        remote(sblock_ref, asked_s.at[1], ask_send.at[0], ask_recv.at[1], (up, col)),
        remote(sblock_ref, asked_s.at[0], ask_send.at[1], ask_recv.at[0], (down, col)),
    ]
    for copy in asks:
        copy.start()

    top, bottom = pl.ds(0, PAD_R), pl.ds(PAD_R + rows, PAD_R)
    mid_c = pl.ds(PAD_C, cols)
    west, east = pl.ds(0, PAD_C), pl.ds(PAD_C + cols, PAD_C)
    all_c = pl.ds(0, cols)
    edge_top, edge_bottom = pl.ds(PAD_R - 1, 1), pl.ds(PAD_R + rows, 1)
    halos = [
        remote(elev_hbm.at[pl.ds(0, 1), all_c], padded.at[edge_bottom, mid_c], halo_send.at[0], halo_recv.at[0], (up, col)),
        remote(
            elev_hbm.at[pl.ds(rows - 1, 1), all_c], padded.at[edge_top, mid_c], halo_send.at[1], halo_recv.at[1], (down, col)
        ),
    ]
    for copy in halos:
        copy.start()
    every_r = pl.ds(0, rows + 2 * PAD_R)
    inner_west, inner_east = pl.ds(PAD_C, PAD_C), pl.ds(cols, PAD_C)
    sides = [
        remote(padded.at[every_r, inner_west], padded.at[every_r, east], halo_send.at[2], halo_recv.at[2], (row, left)),
        remote(padded.at[every_r, inner_east], padded.at[every_r, west], halo_send.at[3], halo_recv.at[3], (row, right)),
    ]
    def clear(where):
        shape = tuple(s.size for s in where)
        padded[where] = jnp.zeros(shape, jnp.float32)

    def first_halo():
        for copy in asks:
            copy.wait_recv()
        halos[0].wait_recv()
        halos[1].wait_recv()

        @pl.when(row == 0)
        def _():
            clear((top, mid_c))

        @pl.when(row == n_row - 1)
        def _():
            clear((bottom, mid_c))

    pool = pooling_matrix()
    bands = rows // BAND
    per_piece = B // BAND
    units = [(step, ORDER[step], half * HALF, HALF) for step in range(2) for half in range(2)]
    units += [(step, m, 0, B) for step, m in enumerate(ORDER) if step > 1]
    half_bands = HALF // BAND
    ahead = 6

    def half_band(i, half):
        return lax.div(i, half_bands) * per_piece + lax.rem(i, half_bands) + half * half_bands

    blind = []

    def send_blind(k):
        for side, (device, place) in enumerate((((up, col), 1), ((down, col), 0))):
            copy = remote(
                blind_send.at[k], blind_got.at[place, k], blind_sems.at[0, side, k], blind_sems.at[1, side, k], device
            )
            copy.start()
            blind.append(copy)

    strips = []
    for unit, (step, m, offset, height) in enumerate(units):
        if unit == 4:
            for copy in sides:
                copy.start()
        if step == 4:
            for copy in sides:
                copy.wait_recv()

            @pl.when(col == 0)
            def _():
                clear((every_r, west))

            @pl.when(col == n_col - 1)
            def _():
                clear((every_r, east))

        lane = pl.multiple_of(sent_col(m) * B, PAD_C)
        slot = step % 2

        def shade_band(i, carry, lane=lane, slot=slot):
            start = pl.multiple_of(i * BAND, BAND)
            cells = padded[pl.ds(start, BAND + 2 * PAD_R), pl.ds(lane, B + 2 * PAD_C)]
            shaded[slot, pl.ds(start, BAND), :] = shade(cells, BAND).astype(jnp.bfloat16)
            return carry

        def first_half(i, carry, shade_band=shade_band):
            return shade_band(half_band(i, 0), carry)

        def second_half(i, carry, shade_band=shade_band):
            return shade_band(half_band(i, 1), carry)

        sent = slice(offset, offset + height)
        if unit == 0:
            for k in range(pieces):
                first_load(k).wait()
                shade_band(k * per_piece + 1, 0)
                rows_k = slice(k * B + BAND, k * B + 2 * BAND)
                blind_send[k] = shaded[slot, rows_k, :]
                if k > 0:
                    send_blind(k - 1)
            for copy in rest:
                copy.start()
            lax.fori_loop(1, pieces, lambda k, c: shade_band(k * per_piece, c), 0)
            send_blind(pieces - 1)
            lax.fori_loop(0, ahead, second_half, 0)
            first_halo()
            shade_band(0, 0)
            sent = slice(0, BAND)
        elif unit == 1:
            lax.fori_loop(ahead, pieces * half_bands, second_half, 0)
        elif unit == 2:
            rest[0].wait()
            rest[1].wait()
            lax.fori_loop(0, pieces * half_bands, first_half, 0, unroll=2)
        elif unit == 3:
            lax.fori_loop(0, pieces * half_bands, second_half, 0, unroll=2)
        else:
            lax.fori_loop(0, bands, shade_band, 0, unroll=2)
        part = slice(offset, offset + height)
        blocks = [slice(k * B + offset, k * B + offset + height) for k in range(pieces)]
        asked_rows = [slice(k * B + sent.start, k * B + sent.stop) for k in range(pieces)]
        for g in range(TR_DEV):
            for side in range(2):
                sendbuf[side, m, g, sent, :] = chosen(
                    lax.div(asked_s[side, 0, g * TC_DEV], TC_DEV), [shaded[slot, k, :] for k in asked_rows]
                )
        for g in range(TR_DEV):
            for side, (device, place) in enumerate((((up, col), 2), ((down, col), 0))):
                sems = (strip_send.at[side, m, g], strip_recv.at[side, m, g])
                if step < 2 and offset == 0:
                    sems = (early_send.at[side, step, g], early_recv.at[side, step, g])
                copy = remote(
                    sendbuf.at[side, m, g, sent, :],
                    recv[m * TR_DEV + g].at[place, sent, :],
                    *sems,
                    device,
                )
                copy.start()
                strips.append(((step, g), copy))
        for g in range(TR_DEV):
            recv[(last - m) * TR_DEV + g][1, part, :] = chosen(
                lax.div(sblock_ref[0, g * TC_DEV], TC_DEV), [shaded[slot, k, :] for k in blocks]
            )
    rest[2].wait()
    rest[3].wait()
    outs = []
    two_copy = remote(two_send, two_got, two_sems.at[0], two_sems.at[1], (row + 1 - 2 * parity, col))

    def out_copy(src, dst):
        copy = pltpu.make_async_copy(src, dst, out_sem.at[len(outs)])
        copy.start()
        outs.append(copy)

    def make_target(g, m):
        j = got_col(m, parity)
        t = g * TC_DEV + j
        place = g * TC_DEV + m
        near = [k for k in (m - 1, m, m + 1) if 0 <= k <= last]
        wanted = lax.rem(sblock_ref[0, t], TC_DEV)
        where = wanted + (1 - parity) * (last - 2 * wanted)
        source = chosen(where - near[0], [merged[g, k] for k in near])
        if (g, m) in LATE:
            spot = LATE.index((g, m))
            late_source[spot] = source
            out_copy(late_source.at[spot], late_out.at[0, spot])
            return
        tile = render(roww[t], source, colw[t])
        sums = []
        for half in range(2):
            tiles[place, half] = tile[:, half * HALF : (half + 1) * HALF]
            lane = pl.multiple_of(j * B + half * HALF, HALF)
            out_copy(tiles.at[place, half], merc_out.at[pl.ds(g * B, B), pl.ds(lane, HALF)])
            sums.append(row_pairs(tiles, (place, half), HALF))
        where = (g * 4 + m // 2, lax.rem(j, 2))
        ones[where] = pooled(jnp.concatenate(sums, axis=1), pool)
        lane = pl.multiple_of(j * HALF, HALF)
        out_copy(ones.at[where], one_out.at[pl.ds(g * HALF, HALF), pl.ds(lane, HALF)])

    def make_coarse(g, pair):
        actual = lax.div(got_col(2 * pair, parity), 2)
        lane = pl.multiple_of(lax.rem(actual, 2) * HALF, HALF)
        sums = [row_pairs(ones, (g * 4 + pair, half), QUARTER) for half in range(2)]
        block = pooled(jnp.concatenate(sums, axis=1), pool)
        where = pl.ds(g * QUARTER, QUARTER), pl.ds(lane, HALF)
        if pair < 2:
            two_send[where] = block.astype(jnp.bfloat16)
        else:
            two_own[where] = block

    for spot, (g, m) in enumerate(LATE):
        t = g * TC_DEV + got_col(m, parity)
        out_copy(roww.at[t], late_out.at[1, spot])
        out_copy(colw.at[t], late_out.at[2, spot])

    done = set()
    for step, m in enumerate(ORDER):
        for g in range(TR_DEV):
            for key, copy in strips:
                if key == (step, g):
                    copy.wait_recv()
            side = srow_ref[0, g * TC_DEV] - row + 1
            if step == 0:
                if g == 0:
                    for copy in blind:
                        copy.wait_recv()
                block = lax.div(sblock_ref[0, g * TC_DEV], TC_DEV)
                rows_b = slice(BAND, 2 * BAND)
                from_up, from_down = (chosen(block, [blind_got[p, k] for k in range(pieces)]) for p in range(2))
                merged[g, m, rows_b, :] = chosen(side, [from_up, recv[m * TR_DEV + g][1, rows_b, :], from_down])
                for rows_b in (slice(0, BAND), slice(2 * BAND, B)):
                    merged[g, m, rows_b, :] = chosen(side, [recv[m * TR_DEV + g][k, rows_b, :] for k in range(3)])
            else:
                merged[g, m] = chosen(side, [recv[m * TR_DEV + g][k] for k in range(3)])
            for target in READY[step]:
                make_target(g, target)
                done.add((g, target))
                pair = target // 2
                both = (g, 2 * pair), (g, 2 * pair + 1)
                if all(x in done and x not in LATE for x in both):
                    make_coarse(g, pair)
        if step == 4:
            two_copy.start()
    out_copy(two_own, two_out)
    two_copy.wait_recv()
    for copy in outs:
        copy.wait()
    two_copy.wait_send()
    for copy in asks + halos + sides + blind + [copy for _, copy in strips]:
        copy.wait_send()


def finish(merc_in, one_in, two_in, two_got, late, merc_hbm, one_hbm, two_hbm, tiles, ones, coarse, other, sem):
    parity = lax.rem(lax.axis_index("row"), 2)
    copies = []

    def start(src, dst):
        copy = pltpu.make_async_copy(src, dst, sem.at[len(copies)])
        copy.start()
        copies.append(copy)

    def same(src, dst, rows, cols):
        start(src.at[rows, cols], dst.at[rows, cols])

    width = TC_DEV * B
    most = 6 * B
    same(merc_in, merc_hbm, pl.ds(0, B), pl.ds(0, width))
    same(merc_in, merc_hbm, pl.ds(B, B), pl.ds(pl.multiple_of((1 - parity) * (width - most), B), most))
    same(one_in, one_hbm, pl.ds(0, HALF), pl.ds(0, width // 2))
    same(one_in, one_hbm, pl.ds(HALF, HALF), pl.ds(pl.multiple_of((1 - parity) * (width - most) // 2, HALF), most // 2))
    own = parity * HALF
    start(two_in.at[pl.ds(0, QUARTER), :], two_hbm.at[pl.ds(pl.multiple_of(own, QUARTER), QUARTER), :])
    low = pl.ds(pl.multiple_of(own + QUARTER, QUARTER), QUARTER)
    lane = pl.ds(pl.multiple_of((1 - parity) * HALF, HALF), HALF)
    start(two_in.at[pl.ds(QUARTER, QUARTER), lane], two_hbm.at[low, lane])
    other[...] = two_got[...].astype(jnp.float32)
    start(other, two_hbm.at[pl.ds(pl.multiple_of((1 - parity) * HALF, HALF), HALF), :])

    pool = pooling_matrix()
    for spot, (g, m) in enumerate(LATE):
        j = got_col(m, parity)
        tile = render(late[1, spot], late[0, spot], late[2, spot])
        sums = []
        for half in range(2):
            tiles[spot, half] = tile[:, half * HALF : (half + 1) * HALF]
            lane = pl.multiple_of(j * B + half * HALF, HALF)
            start(tiles.at[spot, half], merc_hbm.at[pl.ds(g * B, B), pl.ds(lane, HALF)])
            sums.append(row_pairs(tiles, (spot, half), HALF))
        ones[lax.rem(j, 2)] = pooled(jnp.concatenate(sums, axis=1), pool)
        start(ones.at[lax.rem(j, 2)], one_hbm.at[pl.ds(g * HALF, HALF), pl.ds(pl.multiple_of(j * HALF, HALF), HALF)])
    sums = [row_pairs(ones, (half,), QUARTER) for half in range(2)]
    coarse[...] = pooled(jnp.concatenate(sums, axis=1), pool)
    start(coarse, two_hbm.at[low, pl.ds(pl.multiple_of(parity * HALF, HALF), HALF)])
    for copy in copies:
        copy.wait()


def per_device(n_row, n_col, elevation, source_row, source_block, row_weights, col_weights):
    rows, cols = elevation.shape
    targets = source_row.shape[0]
    source_row = source_row.reshape(1, targets)
    source_block = source_block.reshape(1, targets)
    anywhere = pl.BlockSpec(memory_space=pl.ANY)
    in_hbm = pl.BlockSpec(memory_space=pltpu.HBM)
    operands = (source_row, source_block, elevation, row_weights, col_weights)
    vmem, bf16, f32 = pltpu.VMEM, jnp.bfloat16, jnp.float32
    dma = pltpu.SemaphoreType.DMA
    n_out = 3 * targets + 1
    images = (
        jax.ShapeDtypeStruct((TR_DEV * B, TC_DEV * B), f32),
        jax.ShapeDtypeStruct((TR_DEV * HALF, TC_DEV * HALF), f32),
        jax.ShapeDtypeStruct((B, B), f32),
    )
    parts = pl.pallas_call(
        functools.partial(kernel, n_row, n_col),
        out_shape=(
            *images[:2],
            jax.ShapeDtypeStruct((HALF, B), f32),
            jax.ShapeDtypeStruct((HALF, B), bf16),
            jax.ShapeDtypeStruct((3, len(LATE), B, B), bf16),
        ),
        in_specs=[in_hbm] * len(operands),
        out_specs=(anywhere,) * 5,
        scratch_shapes=[
            pltpu.SMEM((1, targets), jnp.int32),
            pltpu.SMEM((1, targets), jnp.int32),
            vmem((rows + 2 * PAD_R, cols + 2 * PAD_C), f32),
            vmem((2, rows, B), bf16),
            pltpu.SMEM((2, 1, targets), jnp.int32),
            vmem((2, TC_DEV, TR_DEV, B, B), bf16),
            vmem((TR_DEV, TC_DEV, B, B), bf16),
            vmem((targets, B, B), bf16),
            vmem((targets, B, B), bf16),
            vmem((targets, 2, B, HALF), f32),
            vmem((targets // 2, 2, HALF, HALF), f32),
            vmem((HALF, B), f32),
            vmem((HALF, B), bf16),
            vmem((len(LATE), B, B), bf16),
            vmem((rows // B, BAND, B), bf16),
            vmem((2, rows // B, BAND, B), bf16),
        ]
        + [vmem((3, B, B), bf16)] * targets
        + [
            dma((rows // B,)), dma((4,)), dma((2, 2, TR_DEV)), dma((2, 2, TR_DEV)),
            dma((2, 2, rows // B)), dma((2,)), dma((2,)), dma((2,)), dma((4,)), dma((4,)),
            dma((2, TC_DEV, TR_DEV)), dma((2, TC_DEV, TR_DEV)), dma((2,)), dma((n_out,)),
        ],
        compiler_params=pltpu.CompilerParams(
            collective_id=0, has_side_effects=True, vmem_limit_bytes=44 * 1024 * 1024
        ),
        name="hillshade_tiles",
    )(*(pltpu.with_memory_space_constraint(x, pltpu.HBM) for x in operands))
    mercator, one, two = pl.pallas_call(
        finish,
        out_shape=images,
        in_specs=[anywhere] * 3 + [pl.BlockSpec(memory_space=vmem)] * 2,
        out_specs=(in_hbm,) * 3,
        scratch_shapes=[
            vmem((len(LATE), 2, B, HALF), f32),
            vmem((2, HALF, HALF), f32),
            vmem((QUARTER, HALF), f32),
            vmem((HALF, B), f32),
            dma((7 + 3 * len(LATE) + 1,)),
        ],
        compiler_params=pltpu.CompilerParams(vmem_limit_bytes=8 * 1024 * 1024),
        name="hillshade_finish",
    )(*parts)
    return mercator, one, two.reshape(1, 1, B, B)


def solution(mesh):
    in_specs = (
        P("row", "col"),
        P(("row", "col"), None),
        P(("row", "col"), None),
        P(("row", "col"), None, None),
        P(("row", "col"), None, None),
    )
    out_specs = (P("row", "col"), P("row", "col"), P("row", "col", None, None))
    return jax.shard_map(
        functools.partial(per_device, mesh.shape["row"], mesh.shape["col"]),
        mesh=mesh, in_specs=in_specs, out_specs=out_specs, check_vma=False,
    )
```

```python
import functools
import math

import jax
import jax.numpy as jnp
from jax import lax
from jax.experimental import pallas as pl
from jax.experimental.pallas import tpu as pltpu
from jax.sharding import PartitionSpec as P

B = 256
HALF = B // 2
QUARTER = B // 4
TR_DEV = 2
TC_DEV = 8
PAD_R = 8
PAD_C = 128
BAND = 64
ORDER = (1, 2, 3, 4, 0, 5, 6, 7)
READY = ((), (), (2,), (3,), (0, 1), (4,), (5,), (6, 7))
LATE = ((1, 6), (1, 7))

SUN_COS = math.cos(math.pi / 4.0)
MESH = pl.DeviceIdType.MESH


def shade(cells, band):
    height, width = cells.shape
    beside = cells + pltpu.roll(cells, width - 1, 1)
    box = beside + pltpu.roll(beside, height - 1, 0)
    box_up = pltpu.roll(box, 1, 0)
    middle = slice(PAD_R, PAD_R + band), slice(PAD_C, width - PAD_C)
    one = box[middle] - pltpu.roll(box_up, 1, 1)[middle]
    two = box_up[middle] - pltpu.roll(box, 1, 1)[middle]
    scale = lax.rsqrt((one * one + two * two) * 32.0 + 1024.0)
    slanted = jnp.maximum(two, -8.0 * SUN_COS) + jnp.maximum(one, -8.0 * SUN_COS)
    straight = jnp.maximum(one + two, -8.0) + jnp.maximum(one - two, -8.0)
    return (straight * SUN_COS + (slanted + 32.0 * SUN_COS)) * scale


def chosen(index, options):
    value = options[0]
    for k, option in enumerate(options[1:], 1):
        value = jnp.where(index == k, option, value)
    return value


def pooled(both, pool):
    high = both.astype(jnp.bfloat16)
    low = (both - high.astype(jnp.float32)).astype(jnp.bfloat16)
    return jnp.dot(high, pool, preferred_element_type=jnp.float32) + jnp.dot(
        low, pool, preferred_element_type=jnp.float32
    )


def got_col(m, parity):
    return (TC_DEV - 1 - m) + parity * (2 * m - (TC_DEV - 1))


def render(row_weights, source, col_weights):
    inner_rows = jnp.dot(row_weights, source, preferred_element_type=jnp.float32).astype(jnp.bfloat16)
    return jnp.dot(inner_rows, col_weights, preferred_element_type=jnp.float32)


def row_pairs(ref, where, count):
    return ref[(*where, pl.ds(0, count, stride=2), slice(None))] + ref[(*where, pl.ds(1, count, stride=2), slice(None))]


def pooling_matrix():
    rows = lax.broadcasted_iota(jnp.int32, (B, HALF), 0)
    cols = lax.broadcasted_iota(jnp.int32, (B, HALF), 1)
    return jnp.where(rows // 2 == cols, 0.25, 0.0).astype(jnp.bfloat16)


def kernel(
    n_row, n_col,
    srow_hbm, ask_hbm, elev_hbm, roww_hbm, colw_hbm,
    merc_out, one_out, two_out, two_got, late_out,
    srow_ref, sblock_ref, padded, shaded, asked_s, sendbuf, merged, roww, colw, tiles, ones, two_own, two_send, late_source, blind_send, blind_got,
    *rest,
):
    recv = rest[:16]
    (first_sem, load_sem, early_send, early_recv, blind_sems, ask_send, ask_recv, ask_local, halo_send, halo_recv,
     strip_send, strip_recv, two_sems, out_sem) = rest[16:]
    row = lax.axis_index("row")
    col = lax.axis_index("col")
    rows, cols = elev_hbm.shape
    parity = lax.rem(row, 2)
    up = lax.rem(row + n_row - 1, n_row)
    down = lax.rem(row + 1, n_row)
    left = lax.rem(col + n_col - 1, n_col)
    right = lax.rem(col + 1, n_col)
    last = TC_DEV - 1

    def sent_col(m):
        return m + parity * (last - 2 * m)

    numbers = [
        pltpu.make_async_copy(srow_hbm, srow_ref, ask_local.at[0]),
        pltpu.make_async_copy(ask_hbm, sblock_ref, ask_local.at[1]),
    ]
    for copy in numbers:
        copy.start()

    around = [(up, col), (down, col), (row, left), (row, right)]
    barrier = pltpu.get_barrier_semaphore()
    for device in around:
        pl.semaphore_signal(barrier, inc=1, device_id=device, device_id_type=MESH)

    pieces = rows // B
    span = B + 2 * PAD_C
    first_lane = pl.multiple_of(sent_col(ORDER[0]) * B - PAD_C, PAD_C)
    narrow, wide = PAD_C, cols - span - PAD_C

    def load(row_start, height, lane, width, sem):
        return pltpu.make_async_copy(
            elev_hbm.at[pl.ds(row_start, height), pl.ds(lane, width)],
            padded.at[pl.ds(row_start + PAD_R, height), pl.ds(lane + PAD_C, width)],
            sem,
        )

    def first_load(i):
        return load(pl.multiple_of(i * B, B), B, first_lane, span, first_sem.at[i])

    for i in range(pieces):
        first_load(i).start()
    rest = [
        load(0, rows, pl.multiple_of((1 - parity) * (narrow + span), PAD_C), wide, load_sem.at[0]),
        load(0, rows, pl.multiple_of(parity * (cols - narrow), PAD_C), narrow, load_sem.at[1]),
        pltpu.make_async_copy(roww_hbm, roww, load_sem.at[2]),
        pltpu.make_async_copy(colw_hbm, colw, load_sem.at[3]),
    ]

    for copy in numbers:
        copy.wait()
    pl.semaphore_wait(barrier, len(around))

    def remote(src, dst, send_sem, recv_sem, device):
        return pltpu.make_async_remote_copy(
            src_ref=src, dst_ref=dst, send_sem=send_sem, recv_sem=recv_sem, device_id=device, device_id_type=MESH
        )

    asks = [
        remote(sblock_ref, asked_s.at[1], ask_send.at[0], ask_recv.at[1], (up, col)),
        remote(sblock_ref, asked_s.at[0], ask_send.at[1], ask_recv.at[0], (down, col)),
    ]
    for copy in asks:
        copy.start()

    top, bottom = pl.ds(0, PAD_R), pl.ds(PAD_R + rows, PAD_R)
    mid_c = pl.ds(PAD_C, cols)
    west, east = pl.ds(0, PAD_C), pl.ds(PAD_C + cols, PAD_C)
    all_c = pl.ds(0, cols)
    edge_top, edge_bottom = pl.ds(PAD_R - 1, 1), pl.ds(PAD_R + rows, 1)
    halos = [
        remote(elev_hbm.at[pl.ds(0, 1), all_c], padded.at[edge_bottom, mid_c], halo_send.at[0], halo_recv.at[0], (up, col)),
        remote(
            elev_hbm.at[pl.ds(rows - 1, 1), all_c], padded.at[edge_top, mid_c], halo_send.at[1], halo_recv.at[1], (down, col)
        ),
    ]
    for copy in halos:
        copy.start()
    every_r = pl.ds(0, rows + 2 * PAD_R)
    inner_west, inner_east = pl.ds(PAD_C, PAD_C), pl.ds(cols, PAD_C)
    sides = [
        remote(padded.at[every_r, inner_west], padded.at[every_r, east], halo_send.at[2], halo_recv.at[2], (row, left)),
        remote(padded.at[every_r, inner_east], padded.at[every_r, west], halo_send.at[3], halo_recv.at[3], (row, right)),
    ]
    def clear(where):
        shape = tuple(s.size for s in where)
        padded[where] = jnp.zeros(shape, jnp.float32)

    def first_halo():
        for copy in asks:
            copy.wait_recv()
        halos[0].wait_recv()
        halos[1].wait_recv()

        @pl.when(row == 0)
        def _():
            clear((top, mid_c))

        @pl.when(row == n_row - 1)
        def _():
            clear((bottom, mid_c))

    pool = pooling_matrix()
    bands = rows // BAND
    per_piece = B // BAND
    units = [(step, ORDER[step], half * HALF, HALF) for step in range(2) for half in range(2)]
    units += [(step, m, 0, B) for step, m in enumerate(ORDER) if step > 1]
    half_bands = HALF // BAND
    ahead = 6

    def half_band(i, half):
        return lax.div(i, half_bands) * per_piece + lax.rem(i, half_bands) + half * half_bands

    blind = []

    def send_blind(k):
        for side, (device, place) in enumerate((((up, col), 1), ((down, col), 0))):
            copy = remote(
                blind_send.at[k], blind_got.at[place, k], blind_sems.at[0, side, k], blind_sems.at[1, side, k], device
            )
            copy.start()
            blind.append(copy)

    strips = []
    for unit, (step, m, offset, height) in enumerate(units):
        if unit == 4:
            for copy in sides:
                copy.start()
        if step == 4:
            for copy in sides:
                copy.wait_recv()

            @pl.when(col == 0)
            def _():
                clear((every_r, west))

            @pl.when(col == n_col - 1)
            def _():
                clear((every_r, east))

        lane = pl.multiple_of(sent_col(m) * B, PAD_C)
        slot = step % 2

        def shade_band(i, carry, lane=lane, slot=slot):
            start = pl.multiple_of(i * BAND, BAND)
            cells = padded[pl.ds(start, BAND + 2 * PAD_R), pl.ds(lane, B + 2 * PAD_C)]
            shaded[slot, pl.ds(start, BAND), :] = shade(cells, BAND).astype(jnp.bfloat16)
            return carry

        def first_half(i, carry, shade_band=shade_band):
            return shade_band(half_band(i, 0), carry)

        def second_half(i, carry, shade_band=shade_band):
            return shade_band(half_band(i, 1), carry)

        sent = slice(offset, offset + height)
        if unit == 0:
            for k in range(pieces):
                first_load(k).wait()
                shade_band(k * per_piece + 1, 0)
                rows_k = slice(k * B + BAND, k * B + 2 * BAND)
                blind_send[k] = shaded[slot, rows_k, :]
                if k > 0:
                    send_blind(k - 1)
            for copy in rest:
                copy.start()
            lax.fori_loop(1, pieces, lambda k, c: shade_band(k * per_piece, c), 0)
            send_blind(pieces - 1)
            lax.fori_loop(0, ahead, second_half, 0)
            first_halo()
            shade_band(0, 0)
            sent = slice(0, BAND)
        elif unit == 1:
            lax.fori_loop(ahead, pieces * half_bands, second_half, 0)
        elif unit == 2:
            rest[0].wait()
            rest[1].wait()
            lax.fori_loop(0, pieces * half_bands, first_half, 0, unroll=2)
        elif unit == 3:
            lax.fori_loop(0, pieces * half_bands, second_half, 0, unroll=2)
        else:
            lax.fori_loop(0, bands, shade_band, 0, unroll=2)
        part = slice(offset, offset + height)
        blocks = [slice(k * B + offset, k * B + offset + height) for k in range(pieces)]
        asked_rows = [slice(k * B + sent.start, k * B + sent.stop) for k in range(pieces)]
        for g in range(TR_DEV):
            for side in range(2):
                sendbuf[side, m, g, sent, :] = chosen(
                    lax.div(asked_s[side, 0, g * TC_DEV], TC_DEV), [shaded[slot, k, :] for k in asked_rows]
                )
        for g in range(TR_DEV):
            for side, (device, place) in enumerate((((up, col), 2), ((down, col), 0))):
                sems = (strip_send.at[side, m, g], strip_recv.at[side, m, g])
                if step < 2 and offset == 0:
                    sems = (early_send.at[side, step, g], early_recv.at[side, step, g])
                copy = remote(
                    sendbuf.at[side, m, g, sent, :],
                    recv[m * TR_DEV + g].at[place, sent, :],
                    *sems,
                    device,
                )
                copy.start()
                strips.append(((step, g), copy))
        for g in range(TR_DEV):
            recv[(last - m) * TR_DEV + g][1, part, :] = chosen(
                lax.div(sblock_ref[0, g * TC_DEV], TC_DEV), [shaded[slot, k, :] for k in blocks]
            )
    rest[2].wait()
    rest[3].wait()
    outs = []
    two_copy = remote(two_send, two_got, two_sems.at[0], two_sems.at[1], (row + 1 - 2 * parity, col))

    def out_copy(src, dst):
        copy = pltpu.make_async_copy(src, dst, out_sem.at[len(outs)])
        copy.start()
        outs.append(copy)

    def make_target(g, m):
        j = got_col(m, parity)
        t = g * TC_DEV + j
        place = g * TC_DEV + m
        near = [k for k in (m - 1, m, m + 1) if 0 <= k <= last]
        wanted = lax.rem(sblock_ref[0, t], TC_DEV)
        where = wanted + (1 - parity) * (last - 2 * wanted)
        source = chosen(where - near[0], [merged[g, k] for k in near])
        if (g, m) in LATE:
            spot = LATE.index((g, m))
            late_source[spot] = source
            out_copy(late_source.at[spot], late_out.at[0, spot])
            return
        tile = render(roww[t], source, colw[t])
        sums = []
        for half in range(2):
            tiles[place, half] = tile[:, half * HALF : (half + 1) * HALF]
            lane = pl.multiple_of(j * B + half * HALF, HALF)
            out_copy(tiles.at[place, half], merc_out.at[pl.ds(g * B, B), pl.ds(lane, HALF)])
            sums.append(row_pairs(tiles, (place, half), HALF))
        where = (g * 4 + m // 2, lax.rem(j, 2))
        ones[where] = pooled(jnp.concatenate(sums, axis=1), pool)
        lane = pl.multiple_of(j * HALF, HALF)
        out_copy(ones.at[where], one_out.at[pl.ds(g * HALF, HALF), pl.ds(lane, HALF)])

    def make_coarse(g, pair):
        actual = lax.div(got_col(2 * pair, parity), 2)
        lane = pl.multiple_of(lax.rem(actual, 2) * HALF, HALF)
        sums = [row_pairs(ones, (g * 4 + pair, half), QUARTER) for half in range(2)]
        block = pooled(jnp.concatenate(sums, axis=1), pool)
        where = pl.ds(g * QUARTER, QUARTER), pl.ds(lane, HALF)
        if pair < 2:
            two_send[where] = block.astype(jnp.bfloat16)
        else:
            two_own[where] = block

    for spot, (g, m) in enumerate(LATE):
        t = g * TC_DEV + got_col(m, parity)
        out_copy(roww.at[t], late_out.at[1, spot])
        out_copy(colw.at[t], late_out.at[2, spot])

    done = set()
    for step, m in enumerate(ORDER):
        for g in range(TR_DEV):
            for key, copy in strips:
                if key == (step, g):
                    copy.wait_recv()
            side = srow_ref[0, g * TC_DEV] - row + 1
            if step == 0:
                if g == 0:
                    for copy in blind:
                        copy.wait_recv()
                block = lax.div(sblock_ref[0, g * TC_DEV], TC_DEV)
                rows_b = slice(BAND, 2 * BAND)
                from_up, from_down = (chosen(block, [blind_got[p, k] for k in range(pieces)]) for p in range(2))
                merged[g, m, rows_b, :] = chosen(side, [from_up, recv[m * TR_DEV + g][1, rows_b, :], from_down])
                for rows_b in (slice(0, BAND), slice(2 * BAND, B)):
                    merged[g, m, rows_b, :] = chosen(side, [recv[m * TR_DEV + g][k, rows_b, :] for k in range(3)])
            else:
                merged[g, m] = chosen(side, [recv[m * TR_DEV + g][k] for k in range(3)])
            for target in READY[step]:
                make_target(g, target)
                done.add((g, target))
                pair = target // 2
                both = (g, 2 * pair), (g, 2 * pair + 1)
                if all(x in done and x not in LATE for x in both):
                    make_coarse(g, pair)
        if step == 4:
            two_copy.start()
    out_copy(two_own, two_out)
    two_copy.wait_recv()
    for copy in outs:
        copy.wait()
    two_copy.wait_send()
    for copy in asks + halos + sides + blind + [copy for _, copy in strips]:
        copy.wait_send()


def finish(merc_in, one_in, two_in, two_got, late, merc_hbm, one_hbm, two_hbm, tiles, ones, coarse, other, sem):
    parity = lax.rem(lax.axis_index("row"), 2)
    copies = []

    def start(src, dst):
        copy = pltpu.make_async_copy(src, dst, sem.at[len(copies)])
        copy.start()
        copies.append(copy)

    def same(src, dst, rows, cols):
        start(src.at[rows, cols], dst.at[rows, cols])

    width = TC_DEV * B
    most = 6 * B
    same(merc_in, merc_hbm, pl.ds(0, B), pl.ds(0, width))
    same(merc_in, merc_hbm, pl.ds(B, B), pl.ds(pl.multiple_of((1 - parity) * (width - most), B), most))
    same(one_in, one_hbm, pl.ds(0, HALF), pl.ds(0, width // 2))
    same(one_in, one_hbm, pl.ds(HALF, HALF), pl.ds(pl.multiple_of((1 - parity) * (width - most) // 2, HALF), most // 2))
    own = parity * HALF
    start(two_in.at[pl.ds(0, QUARTER), :], two_hbm.at[pl.ds(pl.multiple_of(own, QUARTER), QUARTER), :])
    low = pl.ds(pl.multiple_of(own + QUARTER, QUARTER), QUARTER)
    lane = pl.ds(pl.multiple_of((1 - parity) * HALF, HALF), HALF)
    start(two_in.at[pl.ds(QUARTER, QUARTER), lane], two_hbm.at[low, lane])
    other[...] = two_got[...].astype(jnp.float32)
    start(other, two_hbm.at[pl.ds(pl.multiple_of((1 - parity) * HALF, HALF), HALF), :])

    pool = pooling_matrix()
    for spot, (g, m) in enumerate(LATE):
        j = got_col(m, parity)
        tile = render(late[1, spot], late[0, spot], late[2, spot])
        sums = []
        for half in range(2):
            tiles[spot, half] = tile[:, half * HALF : (half + 1) * HALF]
            lane = pl.multiple_of(j * B + half * HALF, HALF)
            start(tiles.at[spot, half], merc_hbm.at[pl.ds(g * B, B), pl.ds(lane, HALF)])
            sums.append(row_pairs(tiles, (spot, half), HALF))
        ones[lax.rem(j, 2)] = pooled(jnp.concatenate(sums, axis=1), pool)
        start(ones.at[lax.rem(j, 2)], one_hbm.at[pl.ds(g * HALF, HALF), pl.ds(pl.multiple_of(j * HALF, HALF), HALF)])
    sums = [row_pairs(ones, (half,), QUARTER) for half in range(2)]
    coarse[...] = pooled(jnp.concatenate(sums, axis=1), pool)
    start(coarse, two_hbm.at[low, pl.ds(pl.multiple_of(parity * HALF, HALF), HALF)])
    for copy in copies:
        copy.wait()


def per_device(n_row, n_col, elevation, source_row, source_block, row_weights, col_weights):
    rows, cols = elevation.shape
    targets = source_row.shape[0]
    source_row = source_row.reshape(1, targets)
    source_block = source_block.reshape(1, targets)
    anywhere = pl.BlockSpec(memory_space=pl.ANY)
    in_hbm = pl.BlockSpec(memory_space=pltpu.HBM)
    operands = (source_row, source_block, elevation, row_weights, col_weights)
    vmem, bf16, f32 = pltpu.VMEM, jnp.bfloat16, jnp.float32
    dma = pltpu.SemaphoreType.DMA
    n_out = 3 * targets + 1
    images = (
        jax.ShapeDtypeStruct((TR_DEV * B, TC_DEV * B), f32),
        jax.ShapeDtypeStruct((TR_DEV * HALF, TC_DEV * HALF), f32),
        jax.ShapeDtypeStruct((B, B), f32),
    )
    parts = pl.pallas_call(
        functools.partial(kernel, n_row, n_col),
        out_shape=(
            *images[:2],
            jax.ShapeDtypeStruct((HALF, B), f32),
            jax.ShapeDtypeStruct((HALF, B), bf16),
            jax.ShapeDtypeStruct((3, len(LATE), B, B), bf16),
        ),
        in_specs=[in_hbm] * len(operands),
        out_specs=(anywhere,) * 5,
        scratch_shapes=[
            pltpu.SMEM((1, targets), jnp.int32),
            pltpu.SMEM((1, targets), jnp.int32),
            vmem((rows + 2 * PAD_R, cols + 2 * PAD_C), f32),
            vmem((2, rows, B), bf16),
            pltpu.SMEM((2, 1, targets), jnp.int32),
            vmem((2, TC_DEV, TR_DEV, B, B), bf16),
            vmem((TR_DEV, TC_DEV, B, B), bf16),
            vmem((targets, B, B), bf16),
            vmem((targets, B, B), bf16),
            vmem((targets, 2, B, HALF), f32),
            vmem((targets // 2, 2, HALF, HALF), f32),
            vmem((HALF, B), f32),
            vmem((HALF, B), bf16),
            vmem((len(LATE), B, B), bf16),
            vmem((rows // B, BAND, B), bf16),
            vmem((2, rows // B, BAND, B), bf16),
        ]
        + [vmem((3, B, B), bf16)] * targets
        + [
            dma((rows // B,)), dma((4,)), dma((2, 2, TR_DEV)), dma((2, 2, TR_DEV)),
            dma((2, 2, rows // B)), dma((2,)), dma((2,)), dma((2,)), dma((4,)), dma((4,)),
            dma((2, TC_DEV, TR_DEV)), dma((2, TC_DEV, TR_DEV)), dma((2,)), dma((n_out,)),
        ],
        compiler_params=pltpu.CompilerParams(
            collective_id=0, has_side_effects=True, vmem_limit_bytes=44 * 1024 * 1024
        ),
        name="hillshade_tiles",
    )(*(pltpu.with_memory_space_constraint(x, pltpu.HBM) for x in operands))
    mercator, one, two = pl.pallas_call(
        finish,
        out_shape=images,
        in_specs=[anywhere] * 3 + [pl.BlockSpec(memory_space=vmem)] * 2,
        out_specs=(in_hbm,) * 3,
        scratch_shapes=[
            vmem((len(LATE), 2, B, HALF), f32),
            vmem((2, HALF, HALF), f32),
            vmem((QUARTER, HALF), f32),
            vmem((HALF, B), f32),
            dma((7 + 3 * len(LATE) + 1,)),
        ],
        compiler_params=pltpu.CompilerParams(vmem_limit_bytes=8 * 1024 * 1024),
        name="hillshade_finish",
    )(*parts)
    return mercator, one, two.reshape(1, 1, B, B)


def solution(mesh):
    in_specs = (
        P("row", "col"),
        P(("row", "col"), None),
        P(("row", "col"), None),
        P(("row", "col"), None, None),
        P(("row", "col"), None, None),
    )
    out_specs = (P("row", "col"), P("row", "col"), P("row", "col", None, None))
    return jax.shard_map(
        functools.partial(per_device, mesh.shape["row"], mesh.shape["col"]),
        mesh=mesh, in_specs=in_specs, out_specs=out_specs, check_vma=False,
    )
```
